512 devices in a mesh: frame: 32 (over x, y), row: 16 (over z, core).
Axes of the slice: x: 4, y: 8, z: 8, core: 2. Of those that a mesh axis runs over, the one named last changes fastest.
Arguments:
- query_tok: bfloat16 [32, 128, 16, 2560], P('frame', 'row'), may hold values from -6 to 6
- key_tok: bfloat16 [32, 128, 16, 2560], P('frame', 'row'), may hold values from -6 to 6
- value_tok: bfloat16 [32, 128, 16, 2560], P('frame', 'row'), may hold values from -6 to 6
- grad_out: bfloat16 [32, 128, 16, 2560], P('frame', 'row'), may hold values from -6 to 6
- head_reach: int32 [20], replicated, may hold values from 0 to 1
- tile_offset: int32 [32, 32], P(None, 'row'), may hold values from -1 to 0
Outputs:
- grad_query: bfloat16 [32, 128, 16, 2560], P('frame', 'row')
- grad_key: bfloat16 [32, 128, 16, 2560], P('frame', 'row')
- grad_value: bfloat16 [32, 128, 16, 2560], P('frame', 'row')
The draws below stay inside these ranges and needn't reach their ends.
All inputs are finite; a program needn't handle non-finite values.
Results may differ from the reference program's by a relative error of at most 0.011.
Values may be sent and summed in bfloat16 or wider, within the bound.
No kernel may reach another device: no remote copies, remote signals or barrier semaphores. Data moves between devices by JAX's collectives and lax.ppermute only.
A program may use at most 64 MiB of HBM per device.

```python
import math
import jax
import jax.numpy as jnp
from jax import lax

HEADS = 20
HEAD_DIM = 128
ROWS_DEV = 8
COLS = 16
FRAMES = 32
ROWS = 128


def drawn(key, which):
    shape = (FRAMES, ROWS, COLS, HEADS * HEAD_DIM)
    own_key = jax.random.fold_in(key, 101 + which)
    values = jnp.clip(jax.random.normal(own_key, shape, jnp.float32), -5.0, 5.0)
    return values.astype(jnp.bfloat16)


def draw_query_tok(key, part):
    return drawn(key, 0)


def draw_key_tok(key, part):
    return drawn(key, 1)


def touch_ends(values, key, smallest, top_value):
    dims = values.shape
    place = [jax.random.randint(jax.random.fold_in(key, axis), (), 0, dims[axis]) for axis in range(len(dims))]
    values = values.at[tuple(place)].set(smallest)
    longest = dims.index(max(dims))
    place[longest] = (place[longest] + 1) % dims[longest]
    return values.at[tuple(place)].set(top_value)


def shard_levels(key, dims, shards, smallest, largest):
    level, own = 1.0, jax.random.fold_in(key, 6)
    for dim, blocks in shards:
        heights = jnp.exp(jax.random.uniform(jax.random.fold_in(own, dim), (blocks,), jnp.float32, smallest / len(shards), largest / len(shards)))
        level = level * jnp.repeat(heights, dims[dim] // blocks).reshape([-1 if axis == dim else 1 for axis in range(len(dims))])
    return level


def noise(rng, extent, scale, limit, pieces=(), kind=jnp.bfloat16):
    values = scale * jax.random.normal(rng, extent, jnp.float32)
    if pieces:
        values = values * shard_levels(rng, extent, pieces, -0.22, 0.18)
    return jnp.clip(values, -limit, limit).astype(kind)


def setup_inputs(seed: int = 0) -> dict:
    arg_keys = jax.random.split(jax.random.key(seed), 7)
    return {
        "query_tok": draw_query_tok(jax.random.fold_in(arg_keys[6], 71), 0),
        "key_tok": draw_key_tok(jax.random.fold_in(arg_keys[6], 71), 0),
        "value_tok": noise(arg_keys[2], (FRAMES, ROWS, COLS, HEADS * HEAD_DIM), 1.0, 6.0, ((0, 32), (1, 16))),
        "grad_out": noise(arg_keys[3], (FRAMES, ROWS, COLS, HEADS * HEAD_DIM), 1.0, 6.0, ((0, 32), (1, 16))),
        "head_reach": touch_ends(jax.random.randint(arg_keys[4], (HEADS,), 0, 2), jax.random.fold_in(arg_keys[4], 1), 0, 1).astype(jnp.int32),
        "tile_offset": touch_ends(jax.random.randint(arg_keys[5], (FRAMES, ROWS // 4), -1, 1), jax.random.fold_in(arg_keys[5], 1), -1, 0).astype(jnp.int32),
    }


def build_windows(padded):
    frame_pad = padded.shape[0]
    rows_in = padded.shape[1] - 4
    tiles = rows_in // 4
    width = padded.shape[2]
    trailing = padded.shape[3:]
    upper_part = padded[:, 0:rows_in].reshape((frame_pad, tiles, 4 * width) + trailing)
    lower_part = padded[:, 4:rows_in + 4].reshape((frame_pad, tiles, 4, width) + trailing)[:, :, 0:2]
    lower_part = lower_part.reshape((frame_pad, tiles, 2 * width) + trailing)
    return jnp.concatenate([upper_part, lower_part], axis=2)

def fold_windows(window_grad, width):
    frame_pad, tiles = (window_grad.shape[0], window_grad.shape[1])
    trailing = window_grad.shape[3:]
    rows_in = 4 * tiles
    tail = [(0, 0)] * len(trailing)
    first = window_grad[:, :, 0:4 * width].reshape((frame_pad, rows_in, width) + trailing)
    second = window_grad[:, :, 4 * width:].reshape((frame_pad, tiles, 2, width) + trailing)
    second = jnp.pad(second, [(0, 0), (0, 0), (0, 2), (0, 0)] + tail).reshape((frame_pad, rows_in, width) + trailing)
    return jnp.pad(first, [(0, 0), (0, 4), (0, 0)] + tail) + jnp.pad(second, [(0, 0), (4, 0), (0, 0)] + tail)

def shift_frames(parts):
    tail = [(0, 0)] * (parts[0].ndim - 1)
    total = jnp.pad(parts[0], [(0, 2)] + tail)
    total = total + jnp.pad(parts[1], [(1, 1)] + tail)
    return total + jnp.pad(parts[2], [(2, 0)] + tail)

def reference(query_tok, key_tok, value_tok, grad_out, head_reach, tile_offset):
    frame_total, row_total, width, packed = query_tok.shape
    heads = head_reach.shape[0]
    head_dim = packed // heads
    tiles = row_total // 4
    inv_root = 1.0 / math.sqrt(head_dim)
    tile_ids = jnp.arange(tiles)[:, None]
    win_rows = jnp.arange(6)[None, :]
    global_row = 4 * tile_ids + win_rows - 1
    offset3 = tile_offset[:, :, None]
    rows_ok = (global_row >= 0) & (global_row < row_total)
    rows_ok = rows_ok[None] & ((win_rows != 0) | (offset3 == -1)) & ((win_rows != 5) | (offset3 == 0))
    rows_ok = jnp.broadcast_to(rows_ok[..., None], rows_ok.shape + (width,)).reshape(frame_total, tiles, 6 * width)
    frame_ids = jnp.arange(frame_total)[:, None] + jnp.arange(3)[None, :] - 1
    frames_ok = (frame_ids >= 0) & (frame_ids < frame_total)
    key_ok = frames_ok[:, None, :, None] & rows_ok[:, :, None, :]
    win_cols = jnp.arange(6 * width) // width
    edge_low = 4 * jnp.arange(tiles) % ROWS_DEV == 0
    edge_high = (4 * jnp.arange(tiles) + 4) % ROWS_DEV == 0
    take_low = (edge_low[:, None] & (win_cols[None, :] == 0))[None, :, :, None, None]
    take_high = (edge_high[:, None] & (win_cols[None, :] == 5))[None, :, :, None, None]

    def one_head(outputs, head):
        grad_q_all, grad_k_all, grad_v_all = outputs
        start = (head * head_dim).astype(jnp.int32)

        def head_slice(array):
            return lax.dynamic_slice_in_dim(array, start, head_dim, 3).astype(jnp.float32)
        query_h = head_slice(query_tok).reshape(frame_total, tiles, 4 * width, head_dim)
        grad_h = head_slice(grad_out).reshape(frame_total, tiles, 4 * width, head_dim)
        pair = jnp.stack([head_slice(key_tok), head_slice(value_tok)], axis=3)
        padded = jnp.pad(pair, ((1, 1), (1, 3), (0, 0), (0, 0), (0, 0)))
        windows = build_windows(padded)
        key_parts = [windows[step:step + frame_total, :, :, 0] for step in range(3)]
        value_parts = [windows[step:step + frame_total, :, :, 1] for step in range(3)]
        heads_ok = (head_reach[head] == 1) | (jnp.arange(3) == 1)
        allowed = key_ok[:, :, None, :, :] & heads_ok[None, None, None, :, None]
        scores = jnp.stack([jnp.einsum('ftqd,ftkd->ftqk', query_h, part) for part in key_parts], axis=3) * inv_root
        scores = jnp.where(allowed, scores, -1e+30)
        top = lax.optimization_barrier(jnp.max(scores, axis=(3, 4), keepdims=True))
        expo = jnp.exp(scores - top)
        probs = expo / lax.optimization_barrier(jnp.sum(expo, axis=(3, 4), keepdims=True))
        weights = probs.astype(jnp.bfloat16).astype(jnp.float32)
        attended = jnp.zeros(query_h.shape, jnp.float32)
        for step in range(3):
            attended = attended + jnp.einsum('ftqk,ftkd->ftqd', weights[:, :, :, step], value_parts[step])
        delta = lax.optimization_barrier(jnp.sum(grad_h * attended, axis=-1))
        dprobs = jnp.stack([jnp.einsum('ftqd,ftkd->ftqk', grad_h, part) for part in value_parts], axis=3)
        dscores = (probs * (dprobs - delta[..., None, None]) * inv_root).astype(jnp.bfloat16).astype(jnp.float32)
        grad_query = jnp.zeros(query_h.shape, jnp.float32)
        pair_parts = []
        for step in range(3):
            grad_query = grad_query + jnp.einsum('ftqk,ftkd->ftqd', dscores[:, :, :, step], key_parts[step])
            key_term = jnp.einsum('ftqk,ftqd->ftkd', dscores[:, :, :, step], query_h)
            value_term = jnp.einsum('ftqk,ftqd->ftkd', weights[:, :, :, step], grad_h)
            pair_parts.append(jnp.stack([key_term, value_term], axis=3))
        spread = shift_frames(pair_parts)
        zeros_f = jnp.zeros_like(spread)
        own_part = fold_windows(jnp.where(take_low | take_high, zeros_f, spread), width)
        low_part = fold_windows(jnp.where(take_low, spread, zeros_f), width)
        high_part = fold_windows(jnp.where(take_high, spread, zeros_f), width)
        own_part = own_part[1:frame_total + 1, 1:row_total + 1]
        low_round = lax.optimization_barrier(low_part[1:frame_total + 1, 1:row_total + 1].astype(jnp.bfloat16))
        high_round = lax.optimization_barrier(high_part[1:frame_total + 1, 1:row_total + 1].astype(jnp.bfloat16))
        pair_total = (own_part + low_round.astype(jnp.float32) + high_round.astype(jnp.float32)).astype(jnp.bfloat16)
        grad_q_head = grad_query.astype(jnp.bfloat16).reshape(frame_total, row_total, width, head_dim)
        grad_q_all = lax.dynamic_update_slice_in_dim(grad_q_all, grad_q_head, start, 3)
        grad_k_all = lax.dynamic_update_slice_in_dim(grad_k_all, pair_total[:, :, :, 0], start, 3)
        grad_v_all = lax.dynamic_update_slice_in_dim(grad_v_all, pair_total[:, :, :, 1], start, 3)
        return ((grad_q_all, grad_k_all, grad_v_all), None)
    empty = jnp.zeros(query_tok.shape, jnp.bfloat16)
    result, _ = lax.scan(one_head, (empty, empty, empty), jnp.arange(heads, dtype=jnp.int32))
    return (result[0], result[1], result[2])
```

```python
import functools
import math

import jax
import jax.numpy as jnp
from jax import lax
from jax.experimental import pallas as pl
from jax.experimental.pallas import tpu as pltpu
from jax.sharding import PartitionSpec as P

STEP = 4
VMEM_LIMIT = 24 << 20
F32, BF16 = jnp.float32, jnp.bfloat16
SMEM = pl.BlockSpec(memory_space=pltpu.SMEM)
VMEM = pl.BlockSpec(memory_space=pltpu.VMEM)
ANY = pl.BlockSpec(memory_space=pl.ANY)


def shifted(block, axis, distance):
    devices = range(lax.axis_size(axis))
    route = [(i - distance, i) for i in devices if i - distance in devices]
    return lax.ppermute(block, axis, route)


def columns(head, dim):
    return pl.ds(pl.multiple_of(head * dim, dim), dim)


def dot_nt(a, b):
    return lax.dot_general(a, b, (((1,), (1,)), ((), ())), preferred_element_type=F32)


def dot_nn(a, b):
    return lax.dot_general(a, b, (((1,), (0,)), ((), ())), preferred_element_type=F32)


def dot_tn(a, b):
    return lax.dot_general(a, b, (((0,), (0,)), ((), ())), preferred_element_type=F32)


class Geometry:
    def __init__(self, tokens, width, dim):
        self.tokens, self.width, self.dim = tokens, width, dim
        self.half = tokens // 2
        self.frames = lax.axis_size("frame")
        self.frame = lax.axis_index("frame")
        self.row = lax.axis_index("row")
        self.rows = lax.axis_size("row")
        self.low_lanes = lax.broadcasted_iota(jnp.int32, (1, tokens), 1) < self.half

    def has(self, frame):
        return (frame >= 0) & (frame < self.frames)

    def offsets(self, offs_ref, frame):
        frame = jnp.clip(frame, 0, self.frames - 1)
        first, second = offs_ref[frame, 0], offs_ref[frame, 1]
        lost0 = (first == -1) & (self.row == 0)
        lost1 = (second == 0) & (self.row == self.rows - 1)
        fine, gone = jnp.float32(0.0), jnp.float32(-1e30)
        penalty = jnp.where(
            self.low_lanes, jnp.where(lost0, gone, fine), jnp.where(lost1, gone, fine)
        )
        return first == -1, second == -1, penalty

    def keys(self, main, low, high, offs):
        half, width = self.half, self.width
        edge0 = jnp.where(offs[0], low, main[half : half + width])
        edge1 = jnp.where(offs[1], main[half - width : half], high)
        return jnp.concatenate([main, edge0, edge1], axis=0)

    def by_tile(self, product):
        half, width, tokens = self.half, self.width, self.tokens
        own = jnp.where(self.low_lanes, product[:half], product[half:tokens])
        edge = jnp.where(
            self.low_lanes, product[tokens : tokens + width], product[tokens + width :]
        )
        return own, edge

    def scores(self, keys, values, query, grad, offs):
        own, edge = self.by_tile(dot_nt(keys, query))
        scale = 1.0 / math.sqrt(self.dim)
        s = jnp.concatenate([own * scale, edge * scale + offs[2]], axis=0)
        dp = jnp.concatenate(self.by_tile(dot_nt(values, grad)), axis=0)
        return s, dp

    def spread(self, terms):
        half = self.half
        own, edge = terms[:half], terms[half:]
        zero_own, zero_edge = jnp.zeros_like(own), jnp.zeros_like(edge)
        low = self.low_lanes
        return jnp.concatenate(
            [
                jnp.where(low, own, zero_own).astype(BF16),
                jnp.where(low, zero_own, own).astype(BF16),
                jnp.where(low, edge, zero_edge).astype(BF16),
                jnp.where(low, zero_edge, edge).astype(BF16),
            ],
            axis=0,
        )

    def grads(self, s, dp, keys, query, grad, top, inverse, delta):
        p = jnp.exp(s - top) * inverse
        ds = p * (dp - delta) * (1.0 / math.sqrt(self.dim))
        weights, dscores = self.spread(p), self.spread(ds)
        return dot_tn(dscores, keys), dot_nn(dscores, query), dot_nn(weights, grad)

    def fold(self, term, offs):
        half, width, tokens = self.half, self.width, self.tokens
        edge0, edge1 = term[tokens : tokens + width], term[tokens + width :]
        none = jnp.zeros_like(edge0)
        main = jnp.concatenate(
            [
                term[: half - width],
                term[half - width : half] + jnp.where(offs[1], edge1, none),
                term[half : half + width] + jnp.where(offs[0], none, edge0),
                term[half + width : tokens],
            ],
            axis=0,
        )
        return main, jnp.where(offs[0], edge0, none), jnp.where(offs[1], none, edge1)


def stats_of(s, dp):
    top = jnp.max(s, axis=0, keepdims=True)
    expo = jnp.exp(s - top)
    return top, jnp.sum(expo, axis=0, keepdims=True), jnp.sum(expo * dp, axis=0, keepdims=True)


def put_stats(ref, pair, side, stats):
    for j, row in enumerate(stats):
        ref[pair, pl.ds(4 * side + j, 1), :] = row


def get_stats(ref, pair, side):
    return [ref[pair, pl.ds(4 * side + j, 1), :] for j in range(3)]


def merge(first, others, valid):
    low = jnp.float32(-1e30)
    tops = [first[0]] + [jnp.where(ok, o[0], low) for o, ok in zip(others, valid)]
    top = functools.reduce(jnp.maximum, tops)
    factor = jnp.exp(first[0] - top)
    total, weighted = first[1] * factor, first[2] * factor
    for o, ok, t in zip(others, valid, tops[1:]):
        factor = jnp.where(ok, jnp.exp(t - top), jnp.float32(0.0))
        total, weighted = total + o[1] * factor, weighted + o[2] * factor
    inverse = 1.0 / total
    return top, inverse, weighted * inverse


def pack_kernel(n, heads, dim, width, reach, q, g, k, v, order, send, low, high, sems):
    tokens = q.shape[0]
    rim_copies = []
    for j, ref in enumerate((k, v)):
        rim_copies.append(pltpu.make_async_copy(ref.at[:width], low.at[j], sems.at[n, j]))
        rim_copies.append(
            pltpu.make_async_copy(ref.at[tokens - width :], high.at[j], sems.at[n + 1, j])
        )
    for copy in rim_copies:
        copy.start()
    count = lax.fori_loop(0, heads, lambda h, c: c + reach[h], 0)

    def place(h, carry):
        on, off = carry
        hit = reach[h] == 1
        order[jnp.where(hit, on, off)] = h
        return jnp.where(hit, on + 1, on), jnp.where(hit, off, off + 1)

    lax.fori_loop(0, heads, place, (0, count))

    def copies(slot):
        cols = columns(order[slot], dim)
        return [
            pltpu.make_async_copy(ref.at[:, cols], send.at[slot, j], sems.at[slot, j])
            for j, ref in enumerate((q, g))
        ]

    def start(slot, carry):
        for copy in copies(slot):
            copy.start()
        return carry

    def wait(slot, carry):
        for copy in copies(slot):
            copy.wait()
        return carry

    lax.fori_loop(0, n, start, 0)
    lax.fori_loop(0, n, wait, 0)
    for copy in rim_copies:
        copy.wait()


def own_kernel(
    n, heads, dim, width, order, offs, q, g, k, v, low, high,
    stats, dq, dk, dv, rim_low, rim_high, buf, rbuf, sems,
):
    geo = Geometry(q.shape[0], width, dim)
    where = geo.offsets(offs, geo.frame)

    def load(slot):
        cols = columns(order[slot], dim)
        keys = geo.keys(k[:, cols], low[0, :, cols], high[0, :, cols], where)
        values = geo.keys(v[:, cols], low[1, :, cols], high[1, :, cols], where)
        return keys, values, q[:, cols], g[:, cols]

    def partial(pair, carry):
        for side in range(2):
            keys, values, query, grad = load(2 * pair + side)
            put_stats(stats, pair, side, stats_of(*geo.scores(keys, values, query, grad, where)))
        return carry

    if n:
        lax.fori_loop(0, n // 2, partial, 0)

    def copies(slot):
        cols = columns(order[slot], dim)
        i = slot - n
        return [
            pltpu.make_async_copy(buf.at[i, j], ref.at[:, cols], sems.at[i, j])
            for j, ref in enumerate((dq, dk, dv))
        ] + [
            pltpu.make_async_copy(rbuf.at[i, j], ref.at[:, :, cols], sems.at[i, 3 + j])
            for j, ref in enumerate((rim_low, rim_high))
        ]

    def finish(pair, carry):
        for side in range(2):
            slot = n + 2 * pair + side
            keys, values, query, grad = load(slot)
            s, dp = geo.scores(keys, values, query, grad, where)
            top, total, weighted = stats_of(s, dp)
            inverse = 1.0 / total
            grad_q, grad_k, grad_v = geo.grads(
                s, dp, keys, query, grad, top, inverse, weighted * inverse
            )
            i = slot - n
            buf[i, 0] = grad_q.astype(BF16)
            for j, term in enumerate((grad_k, grad_v)):
                main, below, above = geo.fold(term, where)
                buf[i, 1 + j] = main.astype(BF16)
                rbuf[i, 0, j] = below.astype(BF16)
                rbuf[i, 1, j] = above.astype(BF16)
            for copy in copies(slot):
                copy.start()
        return carry

    def wait(slot, carry):
        for copy in copies(slot):
            copy.wait()
        return carry

    if n < heads:
        lax.fori_loop(0, (heads - n) // 2, finish, 0)
        lax.fori_loop(n, heads, wait, 0)


def near_kernel(n, dim, width, order, offs, k, v, low, high, prev, following, s_prev, s_next):
    geo = Geometry(k.shape[0], width, dim)

    def pair_step(pair, carry):
        for side in range(2):
            slot = 2 * pair + side
            cols = columns(order[slot], dim)
            for step, near, out in ((-1, prev, s_prev), (1, following, s_next)):
                where = geo.offsets(offs, geo.frame + step)
                keys = geo.keys(k[:, cols], low[0, :, cols], high[0, :, cols], where)
                values = geo.keys(v[:, cols], low[1, :, cols], high[1, :, cols], where)
                s, dp = geo.scores(keys, values, near[slot, 0], near[slot, 1], where)
                put_stats(out, pair, side, stats_of(s, dp))
        return carry

    lax.fori_loop(0, n // 2, pair_step, 0)


def main_kernel(
    n, dim, width, order, reach, offs, q, g, k, v, low, high, prev, following,
    own, own_prev, own_next, near_prev, near_next, at_prev, at_next, far_prev, far_next,
    dk_in, dv_in, rim_low_in, rim_high_in,
    dq_own, dq_prev, dq_next, dk, dv, rim_low, rim_high, buf, rbuf, sems,
):
    del dk_in, dv_in, rim_low_in, rim_high_in
    geo = Geometry(q.shape[0], width, dim)
    f = geo.frame

    def copies(slot):
        cols = columns(order[slot], dim)
        return [
            pltpu.make_async_copy(buf.at[slot, j], ref.at[:, cols], sems.at[slot, j])
            for j, ref in enumerate((dk, dv))
        ] + [
            pltpu.make_async_copy(rbuf.at[slot, j], ref.at[:, :, cols], sems.at[slot, 2 + j])
            for j, ref in enumerate((rim_low, rim_high))
        ]

    def pair_step(pair, carry):
        for side in range(2):
            slot = 2 * pair + side
            head = order[slot]
            on = reach[head] == 1
            cols = columns(head, dim)
            has_prev, has_next = on & geo.has(f - 1), on & geo.has(f + 1)

            def read(ref):
                return get_stats(ref, pair, side)

            merged = {
                0: merge(read(own), [read(at_prev), read(at_next)], [has_prev, has_next]),
                -1: merge(
                    read(near_prev), [read(own_prev), read(far_prev)],
                    [has_prev, on & geo.has(f - 2)],
                ),
                1: merge(
                    read(near_next), [read(own_next), read(far_next)],
                    [has_next, on & geo.has(f + 2)],
                ),
            }
            sources = {
                0: (q[:, cols], g[:, cols]),
                -1: (prev[slot, 0], prev[slot, 1]),
                1: (following[slot, 0], following[slot, 1]),
            }
            folded = []
            for step in (0, -1, 1):
                where = geo.offsets(offs, f + step)
                keys = geo.keys(k[:, cols], low[0, :, cols], high[0, :, cols], where)
                values = geo.keys(v[:, cols], low[1, :, cols], high[1, :, cols], where)
                query, grad = sources[step]
                s, dp = geo.scores(keys, values, query, grad, where)
                top, inverse, delta = merged[step]
                if step:
                    ok = has_prev if step < 0 else has_next
                    inverse = jnp.where(ok, inverse, jnp.float32(0.0))
                grad_q, grad_k, grad_v = geo.grads(
                    s, dp, keys, query, grad, top, inverse, delta
                )
                folded.append([geo.fold(grad_k, where), geo.fold(grad_v, where)])
                if step == 0:
                    dq_own[slot] = grad_q
                else:
                    out = dq_prev if step < 0 else dq_next
                    out[slot] = grad_q.astype(BF16)
            for j in range(2):
                main, below, above = (
                    folded[0][j][part] + folded[1][j][part] + folded[2][j][part]
                    for part in range(3)
                )
                buf[slot, j] = main.astype(BF16)
                rbuf[slot, 0, j] = below.astype(BF16)
                rbuf[slot, 1, j] = above.astype(BF16)
            for copy in copies(slot):
                copy.start()
        return carry

    def wait(slot, carry):
        for copy in copies(slot):
            copy.wait()
        return carry

    lax.fori_loop(0, n // 2, pair_step, 0)
    lax.fori_loop(0, n, wait, 0)


def last_kernel(n, dim, width, order, *refs):
    if n:
        dq_own, at_prev, at_next, below, above, _, _, _, dq, dk, dv, buf, rows, sems, row_sems = refs
    else:
        below, above, _, _, _, dq, dk, dv, buf, rows, sems, row_sems = refs
    tokens = dk.shape[0]
    places = [
        (ref, start, arrived, j)
        for j, ref in enumerate((dk, dv))
        for start, arrived in ((0, below), (tokens - width, above))
    ]

    def row_copies(back):
        made = []
        for i, (ref, start, _, _) in enumerate(places):
            outer, inner = ref.at[pl.ds(start, width)], rows.at[i]
            if back:
                made.append(pltpu.make_async_copy(inner, outer, row_sems.at[i]))
            else:
                made.append(pltpu.make_async_copy(outer, inner, row_sems.at[i]))
        return made

    for copy in row_copies(False):
        copy.start()

    def copy_of(slot):
        return pltpu.make_async_copy(
            buf.at[slot], dq.at[:, columns(order[slot], dim)], sems.at[slot]
        )

    def add(slot, carry):
        total = dq_own[slot] + at_prev[slot].astype(F32) + at_next[slot].astype(F32)
        buf[slot] = total.astype(BF16)
        copy_of(slot).start()
        return carry

    def wait(slot, carry):
        copy_of(slot).wait()
        return carry

    if n:
        lax.fori_loop(0, n, add, 0)
    for copy in row_copies(False):
        copy.wait()
    for i, (_, _, arrived, j) in enumerate(places):
        rows[i] = (rows[i].astype(F32) + arrived[j].astype(F32)).astype(BF16)
    for copy in row_copies(True):
        copy.start()
    if n:
        lax.fori_loop(0, n, wait, 0)
    for copy in row_copies(True):
        copy.wait()


def call(kernel, ins, outs, out_specs, in_specs, scratch, flops, aliases=None, name=None):
    shapes = [jax.ShapeDtypeStruct(s, d) for s, d in outs]
    moved = sum(x.size * x.dtype.itemsize for x in ins)
    return pl.pallas_call(
        kernel,
        out_shape=shapes,
        in_specs=in_specs,
        out_specs=out_specs,
        scratch_shapes=scratch,
        input_output_aliases=aliases or {},
        cost_estimate=pl.CostEstimate(flops=flops, bytes_accessed=moved, transcendentals=0),
        compiler_params=pltpu.CompilerParams(vmem_limit_bytes=VMEM_LIMIT),
        name=name,
    )(*ins)


def run(n, heads, dim, width, args):
    q, g, k, v, reach, offs = args
    tokens, packed = q.shape
    dma = pltpu.SemaphoreType.DMA
    pairs = n // 2
    rim = ((2, width, packed), BF16)
    whole = ((tokens, packed), BF16)
    tile = (tokens, dim)
    flops = 2 * (tokens + 2 * width) * tokens * dim
    if n:
        order, send, low, high = call(
            functools.partial(pack_kernel, n, heads, dim, width),
            [reach, q, g, k, v],
            [((heads,), jnp.int32), ((n, 2) + tile, BF16), rim, rim],
            [SMEM, VMEM, VMEM, VMEM],
            [SMEM] + [ANY] * 4,
            [dma((n + 2, 2))],
            0,
            name="pack",
        )
        prev, following = shifted(send, "frame", 1), shifted(send, "frame", -1)
    else:
        order = jnp.arange(heads, dtype=jnp.int32)
        low = jnp.stack([k[:width], v[:width]])
        high = jnp.stack([k[tokens - width :], v[tokens - width :]])
    low, high = shifted(high, "row", 1), shifted(low, "row", -1)
    stat = ((max(pairs, 1), 8, tokens), F32)
    rest = max(heads - n, 1)
    own, dq, dk, dv, rim_low, rim_high = call(
        functools.partial(own_kernel, n, heads, dim, width),
        [order, offs, q, g, k, v, low, high],
        [stat, whole, whole, whole, rim, rim],
        [VMEM] + [ANY] * 5,
        [SMEM, SMEM] + [VMEM] * 6,
        [
            pltpu.VMEM((rest, 3) + tile, BF16),
            pltpu.VMEM((rest, 2, 2, width, dim), BF16),
            dma((rest, 5)),
        ],
        flops * (2 * n + 5 * (heads - n)),
        name="own",
    )
    if n:
        own_prev, own_next = shifted(own, "frame", 1), shifted(own, "frame", -1)
        near_prev, near_next = call(
            functools.partial(near_kernel, n, dim, width),
            [order, offs, k, v, low, high, prev, following],
            [stat, stat],
            [VMEM] * 2,
            [SMEM, SMEM] + [VMEM] * 6,
            [],
            flops * 4 * n,
            name="near",
        )
        at_prev, at_next = shifted(near_next, "frame", 1), shifted(near_prev, "frame", -1)
        far_prev, far_next = shifted(near_next, "frame", 2), shifted(near_prev, "frame", -2)
        ins = [
            order, reach, offs, q, g, k, v, low, high, prev, following,
            own, own_prev, own_next, near_prev, near_next, at_prev, at_next, far_prev, far_next,
            dk, dv, rim_low, rim_high,
        ]
        dq_own, dq_prev, dq_next, dk, dv, rim_low, rim_high = call(
            functools.partial(main_kernel, n, dim, width),
            ins,
            [((n,) + tile, F32), ((n,) + tile, BF16), ((n,) + tile, BF16), whole, whole, rim, rim],
            [VMEM] * 3 + [ANY] * 4,
            [SMEM] * 3 + [VMEM] * (len(ins) - 7) + [ANY] * 4,
            [
                pltpu.VMEM((n, 2) + tile, BF16),
                pltpu.VMEM((n, 2, 2, width, dim), BF16),
                dma((n, 4)),
            ],
            flops * 15 * n,
            aliases={20: 3, 21: 4, 22: 5, 23: 6},
            name="main",
        )
        back = [dq_own, shifted(dq_next, "frame", 1), shifted(dq_prev, "frame", -1)]
    else:
        back = []
    below, above = shifted(rim_high, "row", 1), shifted(rim_low, "row", -1)
    ins = [order] + back + [below, above, dq, dk, dv]
    at = len(ins) - 3
    return call(
        functools.partial(last_kernel, n, dim, width),
        ins,
        [whole, whole, whole],
        [ANY] * 3,
        [SMEM] + [VMEM] * (at - 1) + [ANY] * 3,
        [
            pltpu.VMEM((max(n, 1),) + tile, BF16),
            pltpu.VMEM((4, width, packed), BF16),
            dma((max(n, 1),)),
            dma((4,)),
        ],
        0,
        aliases={at: 0, at + 1: 1, at + 2: 2},
        name="last",
    )


def on_device(query_tok, key_tok, value_tok, grad_out, head_reach, tile_offset):
    block = query_tok.shape
    rows_dev, width, packed = block[1:]
    heads = head_reach.shape[0]
    dim = packed // heads
    flat = [x.reshape(rows_dev * width, packed) for x in (query_tok, grad_out, key_tok, value_tok)]
    args = flat + [head_reach, tile_offset]
    sizes = list(range(0, heads + 1, STEP))
    count = jnp.sum(head_reach)
    grads = lax.switch(
        (count + STEP - 1) // STEP,
        [functools.partial(run, n, heads, dim, width) for n in sizes],
        args,
    )
    return tuple(x.reshape(block) for x in grads)


def solution(mesh):
    spec = P("frame", "row", None, None)
    return jax.shard_map(
        on_device,
        mesh=mesh,
        in_specs=(spec, spec, spec, spec, P(), P(None, "row")),
        out_specs=(spec, spec, spec),
        check_vma=False,
    )
```

```python
import functools
import math

import jax
import jax.numpy as jnp
from jax import lax
from jax.experimental import pallas as pl
from jax.experimental.pallas import tpu as pltpu
from jax.sharding import PartitionSpec as P

STEP = 4
VMEM_LIMIT = 24 << 20
F32, BF16 = jnp.float32, jnp.bfloat16
SMEM = pl.BlockSpec(memory_space=pltpu.SMEM)
VMEM = pl.BlockSpec(memory_space=pltpu.VMEM)


def shifted(block, axis, distance):
    devices = range(lax.axis_size(axis))
    route = [(i - distance, i) for i in devices if i - distance in devices]
    return lax.ppermute(block, axis, route)


def swapped(block, axis, first):
    count = lax.axis_size(axis)
    pairs = [(i, i + 1) for i in range(first, count - 1, 2)]
    return lax.ppermute(block, axis, pairs + [(b, a) for a, b in pairs])


def columns(head, dim):
    return pl.ds(pl.multiple_of(head * dim, dim), dim)


def dot_nt(a, b):
    return lax.dot_general(a, b, (((1,), (1,)), ((), ())), preferred_element_type=F32)


def dot_nn(a, b):
    return lax.dot_general(a, b, (((1,), (0,)), ((), ())), preferred_element_type=F32)


def dot_tn(a, b):
    return lax.dot_general(a, b, (((0,), (0,)), ((), ())), preferred_element_type=F32)


class Geometry:
    def __init__(self, tokens, width, dim):
        self.tokens, self.width, self.dim = tokens, width, dim
        self.half = tokens // 2
        self.scale = 1.0 / math.sqrt(dim)
        self.frames = lax.axis_size("frame")
        self.frame = lax.axis_index("frame")
        self.row = lax.axis_index("row")
        self.rows = lax.axis_size("row")
        self.even = lax.rem(self.row, 2) == 0
        self.low_lanes = lax.broadcasted_iota(jnp.int32, (1, tokens), 1) < self.half

    def has(self, frame):
        return (frame >= 0) & (frame < self.frames)

    def offsets(self, offs_ref, frame):
        frame = jnp.clip(frame, 0, self.frames - 1)
        first, second = offs_ref[frame, 0], offs_ref[frame, 1]
        lost0 = (first == -1) & (self.row == 0)
        lost1 = (second == 0) & (self.row == self.rows - 1)
        fine, gone = jnp.float32(0.0), jnp.float32(-1e30)
        penalty = jnp.where(
            self.low_lanes, jnp.where(lost0, gone, fine), jnp.where(lost1, gone, fine)
        )
        return first == -1, second == -1, penalty

    def rims(self, near, far):
        return jnp.where(self.even, far, near), jnp.where(self.even, near, far)

    def keys(self, main, low, high, offs):
        half, width = self.half, self.width
        edge0 = jnp.where(offs[0], low, main[half : half + width])
        edge1 = jnp.where(offs[1], main[half - width : half], high)
        return jnp.concatenate([main, edge0, edge1], axis=0)

    def keys_of(self, extended, offs):
        width, end = self.width, self.width + self.tokens
        return self.keys(extended[width:end], extended[:width], extended[end:], offs)

    def by_tile(self, product):
        half, width, tokens = self.half, self.width, self.tokens
        own = jnp.where(self.low_lanes, product[:half], product[half:tokens])
        edge = jnp.where(
            self.low_lanes, product[tokens : tokens + width], product[tokens + width :]
        )
        return own, edge

    def scores(self, keys, values, query, grad, offs):
        own, edge = self.by_tile(dot_nt(keys, query))
        s = jnp.concatenate([own * self.scale, edge * self.scale + offs[2]], axis=0)
        dp = jnp.concatenate(self.by_tile(dot_nt(values, grad)), axis=0)
        return s, dp

    def spread(self, terms):
        half = self.half
        own, edge = terms[:half], terms[half:]
        zero_own, zero_edge = jnp.zeros_like(own), jnp.zeros_like(edge)
        low = self.low_lanes
        return jnp.concatenate(
            [
                jnp.where(low, own, zero_own).astype(BF16),
                jnp.where(low, zero_own, own).astype(BF16),
                jnp.where(low, edge, zero_edge).astype(BF16),
                jnp.where(low, zero_edge, edge).astype(BF16),
            ],
            axis=0,
        )

    def weigh(self, s, dp, top, inverse, delta):
        p = jnp.exp(s - top) * inverse
        ds = p * (dp - delta) * self.scale
        return self.spread(p), self.spread(ds)

    def fold(self, term, offs):
        half, width, tokens = self.half, self.width, self.tokens
        edge0, edge1 = term[tokens : tokens + width], term[tokens + width :]
        none = jnp.zeros_like(edge0)
        return jnp.concatenate(
            [
                jnp.where(offs[0], edge0, none),
                term[: half - width],
                term[half - width : half] + jnp.where(offs[1], edge1, none),
                term[half : half + width] + jnp.where(offs[0], none, edge0),
                term[half + width : tokens],
                jnp.where(offs[1], none, edge1),
            ],
            axis=0,
        )


def stats_of(s, dp):
    top = jnp.max(s, axis=0, keepdims=True)
    expo = jnp.exp(s - top)
    return top, jnp.sum(expo, axis=0, keepdims=True), jnp.sum(expo * dp, axis=0, keepdims=True)


def put_stats(ref, pair, side, stats):
    for j, row in enumerate(stats):
        ref[pair, pl.ds(4 * side + j, 1), :] = row


def get_stats(ref, pair, side):
    return [ref[pair, pl.ds(4 * side + j, 1), :] for j in range(3)]


def merge(first, others, valid):
    low = jnp.float32(-1e30)
    tops = [first[0]] + [jnp.where(ok, o[0], low) for o, ok in zip(others, valid)]
    top = functools.reduce(jnp.maximum, tops)
    factor = jnp.exp(first[0] - top)
    total, weighted = first[1] * factor, first[2] * factor
    for o, ok, t in zip(others, valid, tops[1:]):
        factor = jnp.where(ok, jnp.exp(t - top), jnp.float32(0.0))
        total, weighted = total + o[1] * factor, weighted + o[2] * factor
    inverse = 1.0 / total
    return top, inverse, weighted * inverse


def edge_kernel(heads, width, reach, k, v, order, near, far):
    tokens = k.shape[0]
    even = lax.rem(lax.axis_index("row"), 2) == 0
    for j, ref in enumerate((k, v)):
        first, last = ref[:width], ref[tokens - width :]
        near[j] = jnp.where(even, last, first)
        far[j] = jnp.where(even, first, last)
    count = lax.fori_loop(0, heads, lambda h, c: c + reach[h], 0)

    def place(h, carry):
        on, off = carry
        hit = reach[h] == 1
        order[jnp.where(hit, on, off)] = h
        return jnp.where(hit, on + 1, on), jnp.where(hit, off, off + 1)

    lax.fori_loop(0, heads, place, (0, count))


def pack_kernel(n, dim, order, q, g, send):
    for slot in range(n):
        cols = columns(order[slot], dim)
        send[slot, 0] = q[:, cols]
        send[slot, 1] = g[:, cols]


def extend_kernel(n, dim, width, order, k, v, near, far, send):
    tokens = k.shape[0]
    geo = Geometry(tokens, width, dim)
    for slot in range(n):
        cols = columns(order[slot], dim)
        for j, ref in enumerate((k, v)):
            low, high = geo.rims(near[j, :, cols], far[j, :, cols])
            send[slot, j, :width] = low
            send[slot, j, width : width + tokens] = ref[:, cols]
            send[slot, j, width + tokens :] = high


def own_kernel(n, heads, dim, width, order, offs, q, g, k, v, near, far, grads, rims):
    tokens = q.shape[0]
    geo = Geometry(tokens, width, dim)
    where = geo.offsets(offs, geo.frame)

    def finish(pair, carry):
        for side in range(2):
            i = 2 * pair + side
            cols = columns(order[n + i], dim)
            low, high = geo.rims(near[0, :, cols], far[0, :, cols])
            keys = geo.keys(k[:, cols], low, high, where)
            low, high = geo.rims(near[1, :, cols], far[1, :, cols])
            values = geo.keys(v[:, cols], low, high, where)
            query, grad = q[:, cols], g[:, cols]
            s, dp = geo.scores(keys, values, query, grad, where)
            top, total, weighted = stats_of(s, dp)
            inverse = 1.0 / total
            weights, dscores = geo.weigh(s, dp, top, inverse, weighted * inverse)
            grads[i, 0] = dot_tn(dscores, keys).astype(BF16)
            for j, term in enumerate((dot_nn(dscores, query), dot_nn(weights, grad))):
                folded = geo.fold(term, where)
                grads[i, 1 + j] = folded[width : width + tokens].astype(BF16)
                rims[i, 0, j] = folded[:width].astype(BF16)
                rims[i, 1, j] = folded[width + tokens :].astype(BF16)
        return carry

    lax.fori_loop(0, (heads - n) // 2, finish, 0)


def query_kernel(n, dim, width, order, reach, offs, own_q, own, prev, following, stats, s_out, dp_out):
    geo = Geometry(own_q.shape[2], width, dim)
    where = geo.offsets(offs, geo.frame)
    has_prev, has_next = geo.has(geo.frame - 1), geo.has(geo.frame + 1)

    def pair_step(pair, carry):
        for side in range(2):
            slot = 2 * pair + side
            on = reach[order[slot]] == 1
            parts = []
            for i, block in enumerate((own, prev, following)):
                keys = geo.keys_of(block[slot, 0], where)
                values = geo.keys_of(block[slot, 1], where)
                s, dp = geo.scores(keys, values, own_q[slot, 0], own_q[slot, 1], where)
                s_out[slot, i] = s
                dp_out[slot, i] = dp
                parts.append(stats_of(s, dp))
            put_stats(stats, pair, side, merge(parts[0], parts[1:], [on & has_prev, on & has_next]))
        return carry

    lax.fori_loop(0, n // 2, pair_step, 0)


def finish_kernel(
    n, dim, width, order, reach, offs, own_q, own, prev, following, stats, s_in, dp_in, acc, dq
):
    geo = Geometry(own_q.shape[2], width, dim)
    where = geo.offsets(offs, geo.frame)
    has_prev, has_next = geo.has(geo.frame - 1), geo.has(geo.frame + 1)

    def pair_step(pair, carry):
        for side in range(2):
            slot = 2 * pair + side
            on = reach[order[slot]] == 1
            top, inverse, delta = get_stats(stats, pair, side)
            total = None
            for i, (block, ok) in enumerate(
                ((own, None), (prev, on & has_prev), (following, on & has_next))
            ):
                keys = geo.keys_of(block[slot, 0], where)
                part = inverse if ok is None else jnp.where(ok, inverse, jnp.float32(0.0))
                s = s_in[slot, i] if ok is None else jnp.minimum(s_in[slot, i], top)
                weights, dscores = geo.weigh(s, dp_in[slot, i], top, part, delta)
                term = dot_tn(dscores, keys)
                total = term if total is None else total + term
                if ok is None:
                    acc[slot, 0] = geo.fold(dot_nn(dscores, own_q[slot, 0]), where)
                    acc[slot, 1] = geo.fold(dot_nn(weights, own_q[slot, 1]), where)
            dq[slot] = total.astype(BF16)
        return carry

    lax.fori_loop(0, n // 2, pair_step, 0)


def key_kernel(
    n, dim, width, order, reach, offs, own, q_prev, q_next, st_prev, st_next, acc, *refs
):
    tokens = q_prev.shape[2]
    geo = Geometry(tokens, width, dim)
    others, (grads, rim_low, rim_high) = refs[:-3], refs[-3:]

    def pair_step(pair, carry):
        for side in range(2):
            slot = 2 * pair + side
            head = order[slot]
            on = reach[head] == 1
            total = [acc[slot, 0], acc[slot, 1]]
            for step, queries, stats in ((-1, q_prev, st_prev), (1, q_next, st_next)):
                where = geo.offsets(offs, geo.frame + step)
                keys = geo.keys_of(own[slot, 0], where)
                values = geo.keys_of(own[slot, 1], where)
                query, grad = queries[slot, 0], queries[slot, 1]
                s, dp = geo.scores(keys, values, query, grad, where)
                top, inverse, delta = get_stats(stats, pair, side)
                ok = on & geo.has(geo.frame + step)
                inverse = jnp.where(ok, inverse, jnp.float32(0.0))
                weights, dscores = geo.weigh(jnp.minimum(s, top), dp, top, inverse, delta)
                total[0] = total[0] + geo.fold(dot_nn(dscores, query), where)
                total[1] = total[1] + geo.fold(dot_nn(weights, grad), where)
            cols = columns(head, dim)
            for j in range(2):
                grads[slot, j] = total[j][width : width + tokens].astype(BF16)
                rim_low[j, :, cols] = total[j][:width].astype(BF16)
                rim_high[j, :, cols] = total[j][width + tokens :].astype(BF16)
        return carry

    lax.fori_loop(0, n // 2, pair_step, 0)
    if others:
        spread_rims(n, order, others[0], rim_low, rim_high, dim)


def spread_rims(n, order, rims, rim_low, rim_high, dim):
    for i in range(rims.shape[0]):
        cols = columns(order[n + i], dim)
        for j in range(2):
            rim_low[j, :, cols] = rims[i, 0, j]
            rim_high[j, :, cols] = rims[i, 1, j]


def rim_kernel(dim, order, rims, rim_low, rim_high):
    spread_rims(0, order, rims, rim_low, rim_high, dim)


def query_out_kernel(n, dim, order, *refs):
    parts, out = refs[:-1], refs[-1]
    for slot in range(n):
        out[:, columns(order[slot], dim)] = parts[0][slot]
    if len(parts) > bool(n):
        for i in range(parts[-1].shape[0]):
            out[:, columns(order[n + i], dim)] = parts[-1][i, 0]


def last_kernel(n, dim, width, order, below, above, *refs):
    parts, outs = refs[:-2], refs[-2:]
    tokens = outs[0].shape[0]

    def put(j, head, ref, i, at):
        cols = columns(head, dim)
        out = outs[j]
        low = ref[i, at, :width].astype(F32) + below[j, :, cols].astype(F32)
        high = ref[i, at, tokens - width :].astype(F32) + above[j, :, cols].astype(F32)
        out[:width, cols] = low.astype(BF16)
        out[width : tokens - width, cols] = ref[i, at, width : tokens - width]
        out[tokens - width :, cols] = high.astype(BF16)

    for j in range(2):
        for slot in range(n):
            put(j, order[slot], parts[0], slot, j)
        if len(parts) > bool(n):
            for i in range(parts[-1].shape[0]):
                put(j, order[n + i], parts[-1], i, 1 + j)


def call(name, kernel, ins, outs, flops):
    shapes = [jax.ShapeDtypeStruct(s, d) for s, d in outs]
    moved = sum(x.size * x.dtype.itemsize for x in list(ins) + shapes)
    return pl.pallas_call(
        kernel,
        out_shape=shapes,
        in_specs=[SMEM if x.dtype == jnp.int32 else VMEM for x in ins],
        out_specs=[SMEM if x.dtype == jnp.int32 else VMEM for x in shapes],
        cost_estimate=pl.CostEstimate(flops=flops, bytes_accessed=moved, transcendentals=0),
        compiler_params=pltpu.CompilerParams(vmem_limit_bytes=VMEM_LIMIT),
        name=name,
    )(*ins)


def run(n, heads, dim, width, args):
    q, g, k, v, reach, offs = args
    tokens, packed = q.shape
    part = functools.partial
    rim = ((2, width, packed), BF16)
    whole = ((tokens, packed), BF16)
    tile = (tokens, dim)
    longer = (tokens + 2 * width, dim)
    flops = 2 * longer[0] * tokens * dim
    rest = heads - n
    order, near, far = call(
        "edge", part(edge_kernel, heads, width), [reach, k, v],
        [((heads,), jnp.int32), rim, rim], 0,
    )
    near, far = swapped(near, "row", 0), swapped(far, "row", 1)
    grads_own = rims = None
    if n:
        (own,) = call(
            "extend", part(extend_kernel, n, dim, width), [order, k, v, near, far],
            [((n, 2) + longer, BF16)], 0,
        )
        prev, following = shifted(own, "frame", 1), shifted(own, "frame", -1)
        (own_q,) = call(
            "pack", part(pack_kernel, n, dim), [order, q, g], [((n, 2) + tile, BF16)], 0
        )
        q_prev, q_next = shifted(own_q, "frame", 1), shifted(own_q, "frame", -1)
    if rest:
        grads_own, rims = call(
            "own", part(own_kernel, n, heads, dim, width), [order, offs, q, g, k, v, near, far],
            [((rest, 3) + tile, BF16), ((rest, 2, 2, width, dim), BF16)], flops * 5 * rest,
        )
    more = [grads_own] if rest else []
    if n:
        grid = ((n, 3, tokens // 2 + width, tokens), F32)
        stats, s, dp = call(
            "query", part(query_kernel, n, dim, width),
            [order, reach, offs, own_q, own, prev, following],
            [((n // 2, 8, tokens), F32), grid, grid], flops * 6 * n,
        )
        st_prev, st_next = shifted(stats, "frame", 1), shifted(stats, "frame", -1)
        acc, dq = call(
            "finish", part(finish_kernel, n, dim, width),
            [order, reach, offs, own_q, own, prev, following, stats, s, dp],
            [((n, 2) + longer, F32), ((n,) + tile, BF16)], flops * 5 * n,
        )
        grads, rim_low, rim_high = call(
            "key", part(key_kernel, n, dim, width),
            [order, reach, offs, own, q_prev, q_next, st_prev, st_next, acc]
            + ([rims] if rest else []),
            [((n, 2) + tile, BF16), rim, rim], flops * 8 * n,
        )
        query_parts, key_parts = [dq] + more, [grads] + more
    else:
        rim_low, rim_high = call("rims", part(rim_kernel, dim), [order, rims], [rim, rim], 0)
        query_parts = key_parts = more
    below, above = shifted(rim_high, "row", 1), shifted(rim_low, "row", -1)
    (dq,) = call("dq", part(query_out_kernel, n, dim), [order] + query_parts, [whole], 0)
    dk, dv = call(
        "last", part(last_kernel, n, dim, width), [order, below, above] + key_parts,
        [whole, whole], 0,
    )
    return dq, dk, dv


def on_device(query_tok, key_tok, value_tok, grad_out, head_reach, tile_offset):
    block = query_tok.shape
    rows_dev, width, packed = block[1:]
    heads = head_reach.shape[0]
    dim = packed // heads
    flat = [x.reshape(rows_dev * width, packed) for x in (query_tok, grad_out, key_tok, value_tok)]
    args = flat + [head_reach, tile_offset]
    sizes = list(range(0, heads + 1, STEP))
    count = jnp.sum(head_reach)
    grads = lax.switch(
        (count + STEP - 1) // STEP,
        [functools.partial(run, n, heads, dim, width) for n in sizes],
        args,
    )
    return tuple(x.reshape(block) for x in grads)


def solution(mesh):
    spec = P("frame", "row", None, None)
    return jax.shard_map(
        on_device,
        mesh=mesh,
        in_specs=(spec, spec, spec, spec, P(), P(None, "row")),
        out_specs=(spec, spec, spec),
        check_vma=False,
    )
```

```python
import functools
import math

import jax
import jax.numpy as jnp
from jax import lax
from jax.experimental import pallas as pl
from jax.experimental.pallas import tpu as pltpu
from jax.sharding import PartitionSpec as P


SIZES = (4, 6, 8, 10, 12, 14, 16, 20)
VMEM_LIMIT = 16 << 20
F32, BF16 = jnp.float32, jnp.bfloat16
SMEM = pl.BlockSpec(memory_space=pltpu.SMEM)
VMEM = pl.BlockSpec(memory_space=pltpu.VMEM)


def both(block):
    return shifted(block, "frame", 1), shifted(block, "frame", -1)


def shifted(block, axis, distance):
    devices = range(lax.axis_size(axis))
    route = [(i - distance, i) for i in devices if i - distance in devices]
    return lax.ppermute(block, axis, route)


def swapped(block, axis, first):
    count = lax.axis_size(axis)
    pairs = [(i, i + 1) for i in range(first, count - 1, 2)]
    return lax.ppermute(block, axis, pairs + [(b, a) for a, b in pairs])


def columns(head, dim):
    return pl.ds(pl.multiple_of(head * dim, dim), dim)


def dot_nt(a, b):
    return lax.dot_general(a, b, (((1,), (1,)), ((), ())), preferred_element_type=F32)


def dot_nn(a, b):
    return lax.dot_general(a, b, (((1,), (0,)), ((), ())), preferred_element_type=F32)


def dot_tn(a, b):
    return lax.dot_general(a, b, (((0,), (0,)), ((), ())), preferred_element_type=F32)


class Geometry:
    def __init__(self, tokens, width, dim):
        self.tokens, self.width, self.dim = tokens, width, dim
        self.half = tokens // 2
        self.scale = 1.0 / math.sqrt(dim)
        self.frames = lax.axis_size("frame")
        self.frame = lax.axis_index("frame")
        self.row = lax.axis_index("row")
        self.rows = lax.axis_size("row")
        self.even = lax.rem(self.row, 2) == 0
        self.low_lanes = lax.broadcasted_iota(jnp.int32, (1, tokens), 1) < self.half

    def has(self, frame):
        return (frame >= 0) & (frame < self.frames)

    def offsets(self, offs_ref, frame):
        frame = jnp.clip(frame, 0, self.frames - 1)
        first, second = offs_ref[frame, 0], offs_ref[frame, 1]
        lost0 = (first == -1) & (self.row == 0)
        lost1 = (second == 0) & (self.row == self.rows - 1)
        fine, gone = jnp.float32(0.0), jnp.float32(-1e30)
        penalty = jnp.where(
            self.low_lanes, jnp.where(lost0, gone, fine), jnp.where(lost1, gone, fine)
        )
        return first == -1, second == -1, penalty

    def rims(self, near, far):
        return jnp.where(self.even, far, near), jnp.where(self.even, near, far)

    def keys(self, main, low, high, offs):
        half, width = self.half, self.width
        edge0 = jnp.where(offs[0], low, main[half : half + width])
        edge1 = jnp.where(offs[1], main[half - width : half], high)
        return jnp.concatenate([main, edge0, edge1], axis=0)

    def keys_of(self, main, rims, slot, j, offs):
        return self.keys(main[slot, j], rims[slot, j, 0], rims[slot, j, 1], offs)

    def by_tile(self, product):
        half, width, tokens = self.half, self.width, self.tokens
        own = jnp.where(self.low_lanes, product[:half], product[half:tokens])
        edge = jnp.where(
            self.low_lanes, product[tokens : tokens + width], product[tokens + width :]
        )
        return own, edge

    def scores(self, keys, values, query, grad, offs):
        own, edge = self.by_tile(dot_nt(keys, query))
        s = jnp.concatenate([own * self.scale, edge * self.scale + offs[2]], axis=0)
        dp = jnp.concatenate(self.by_tile(dot_nt(values, grad)), axis=0)
        return s, dp

    def spread(self, terms):
        half = self.half
        own, edge = terms[:half], terms[half:]
        zero_own, zero_edge = jnp.zeros_like(own), jnp.zeros_like(edge)
        low = self.low_lanes
        return jnp.concatenate(
            [
                jnp.where(low, own, zero_own).astype(BF16),
                jnp.where(low, zero_own, own).astype(BF16),
                jnp.where(low, edge, zero_edge).astype(BF16),
                jnp.where(low, zero_edge, edge).astype(BF16),
            ],
            axis=0,
        )

    def weigh(self, s, dp, top, inverse, delta):
        p = jnp.exp(s - top) * inverse
        ds = p * (dp - delta) * self.scale
        return self.spread(p), self.spread(ds)

    def fold(self, term, offs):
        half, width, tokens = self.half, self.width, self.tokens
        edge0, edge1 = term[tokens : tokens + width], term[tokens + width :]
        none = jnp.zeros_like(edge0)
        return jnp.concatenate(
            [
                jnp.where(offs[0], edge0, none),
                term[: half - width],
                term[half - width : half] + jnp.where(offs[1], edge1, none),
                term[half : half + width] + jnp.where(offs[0], none, edge0),
                term[half + width : tokens],
                jnp.where(offs[1], none, edge1),
            ],
            axis=0,
        )


def stats_of(s, dp):
    top = jnp.max(s, axis=0, keepdims=True)
    expo = jnp.exp(s - top)
    return top, jnp.sum(expo, axis=0, keepdims=True), jnp.sum(expo * dp, axis=0, keepdims=True)


def put_stats(ref, pair, side, stats):
    for j, row in enumerate(stats):
        ref[pair, pl.ds(4 * side + j, 1), :] = row


def get_stats(ref, pair, side):
    return [ref[pair, pl.ds(4 * side + j, 1), :] for j in range(3)]


def merge(first, others, valid):
    low = jnp.float32(-1e30)
    tops = [first[0]] + [jnp.where(ok, o[0], low) for o, ok in zip(others, valid)]
    top = functools.reduce(jnp.maximum, tops)
    factor = jnp.exp(first[0] - top)
    total, weighted = first[1] * factor, first[2] * factor
    for o, ok, t in zip(others, valid, tops[1:]):
        factor = jnp.where(ok, jnp.exp(t - top), jnp.float32(0.0))
        total, weighted = total + o[1] * factor, weighted + o[2] * factor
    inverse = 1.0 / total
    return top, inverse, weighted * inverse


def each(count, body):
    def step(i, carry):
        body(i)
        return carry

    lax.fori_loop(0, count, step, 0)


def first_kernel(n, heads, dim, width, reach, k, v, order, near, far, *rest):
    tokens = k.shape[0]
    even = lax.rem(lax.axis_index("row"), 2) == 0
    count = lax.fori_loop(0, heads, lambda h, c: c + reach[h], 0)

    def place(h, carry):
        on, off = carry
        hit = reach[h] == 1
        order[jnp.where(hit, on, off)] = h
        return jnp.where(hit, on + 1, on), jnp.where(hit, off, off + 1)

    lax.fori_loop(0, heads, place, (0, count))

    def pack(slot):
        cols = columns(order[slot], dim)
        for j, ref in enumerate((k, v)):
            rest[0][slot, j] = ref[:, cols]

    if n:
        each(n, pack)
    for j, ref in enumerate((k, v)):
        first, last = ref[:width], ref[tokens - width :]
        near[j] = jnp.where(even, last, first)
        far[j] = jnp.where(even, first, last)


def pack_kernel(n, dim, order, q, g, rims, send):
    del rims

    def pack(slot):
        cols = columns(order[slot], dim)
        send[slot, 0] = q[:, cols]
        send[slot, 1] = g[:, cols]

    each(n, pack)


def rims_kernel(n, dim, width, order, near, far, send):
    geo = Geometry(8 * width, width, dim)

    def pack(slot):
        cols = columns(order[slot], dim)
        for j in range(2):
            low, high = geo.rims(near[j, :, cols], far[j, :, cols])
            send[slot, j, 0] = low
            send[slot, j, 1] = high

    each(n, pack)


def own_kernel(n, heads, dim, width, order, offs, q, g, k, v, near, far, grads, rims):
    tokens = q.shape[0]
    geo = Geometry(tokens, width, dim)
    where = geo.offsets(offs, geo.frame)

    def finish(pair, carry):
        for side in range(2):
            i = 2 * pair + side
            cols = columns(order[n + i], dim)
            low, high = geo.rims(near[0, :, cols], far[0, :, cols])
            keys = geo.keys(k[:, cols], low, high, where)
            low, high = geo.rims(near[1, :, cols], far[1, :, cols])
            values = geo.keys(v[:, cols], low, high, where)
            query, grad = q[:, cols], g[:, cols]
            s, dp = geo.scores(keys, values, query, grad, where)
            top, total, weighted = stats_of(s, dp)
            inverse = 1.0 / total
            weights, dscores = geo.weigh(s, dp, top, inverse, weighted * inverse)
            grads[i, 0] = dot_tn(dscores, keys).astype(BF16)
            for j, term in enumerate((dot_nn(dscores, query), dot_nn(weights, grad))):
                folded = geo.fold(term, where)
                grads[i, 1 + j] = folded[width : width + tokens].astype(BF16)
                rims[i, 0, j] = folded[:width].astype(BF16)
                rims[i, 1, j] = folded[width + tokens :].astype(BF16)
        return carry

    lax.fori_loop(0, (heads - n) // 2, finish, 0)


def query_kernel(
    n, dim, width, order, reach, offs, own_q, own, prev, following,
    own_r, prev_r, next_r, stats, s_out, dp_out,
):
    geo = Geometry(own_q.shape[2], width, dim)
    where = geo.offsets(offs, geo.frame)
    has_prev, has_next = geo.has(geo.frame - 1), geo.has(geo.frame + 1)

    def pair_step(pair, carry):
        for side in range(2):
            slot = 2 * pair + side
            on = reach[order[slot]] == 1
            parts = []
            for i, (block, rims) in enumerate(
                ((own, own_r), (prev, prev_r), (following, next_r))
            ):
                keys = geo.keys_of(block, rims, slot, 0, where)
                values = geo.keys_of(block, rims, slot, 1, where)
                s, dp = geo.scores(keys, values, own_q[slot, 0], own_q[slot, 1], where)
                s_out[slot, i] = s
                dp_out[slot, i] = dp
                parts.append(stats_of(s, dp))
            put_stats(stats, pair, side, merge(parts[0], parts[1:], [on & has_prev, on & has_next]))
        return carry

    lax.fori_loop(0, n // 2, pair_step, 0)


def finish_kernel(
    n, dim, width, order, reach, offs, own_q, own, prev, following,
    own_r, prev_r, next_r, stats, s_in, dp_in, acc, dq,
):
    geo = Geometry(own_q.shape[2], width, dim)
    where = geo.offsets(offs, geo.frame)
    has_prev, has_next = geo.has(geo.frame - 1), geo.has(geo.frame + 1)

    def pair_step(pair, carry):
        for side in range(2):
            slot = 2 * pair + side
            on = reach[order[slot]] == 1
            top, inverse, delta = get_stats(stats, pair, side)
            total = None
            for i, (block, rims, ok) in enumerate(
                (
                    (own, own_r, None),
                    (prev, prev_r, on & has_prev),
                    (following, next_r, on & has_next),
                )
            ):
                keys = geo.keys_of(block, rims, slot, 0, where)
                part = inverse if ok is None else jnp.where(ok, inverse, jnp.float32(0.0))
                s = s_in[slot, i] if ok is None else jnp.minimum(s_in[slot, i], top)
                weights, dscores = geo.weigh(s, dp_in[slot, i], top, part, delta)
                term = dot_tn(dscores, keys)
                total = term if total is None else total + term
                if ok is None:
                    acc[slot, 0] = geo.fold(dot_nn(dscores, own_q[slot, 0]), where)
                    acc[slot, 1] = geo.fold(dot_nn(weights, own_q[slot, 1]), where)
            dq[slot] = total.astype(BF16)
        return carry

    lax.fori_loop(0, n // 2, pair_step, 0)


def key_kernel(
    n, dim, width, order, reach, offs, own, own_r, q_prev, q_next, st_prev, st_next, acc, *refs
):
    tokens = q_prev.shape[2]
    geo = Geometry(tokens, width, dim)
    others, (grads, rim_low, rim_high) = refs[:-3], refs[-3:]

    def pair_step(pair, carry):
        for side in range(2):
            slot = 2 * pair + side
            head = order[slot]
            on = reach[head] == 1
            total = [acc[slot, 0], acc[slot, 1]]
            for step, queries, stats in ((-1, q_prev, st_prev), (1, q_next, st_next)):
                where = geo.offsets(offs, geo.frame + step)
                keys = geo.keys_of(own, own_r, slot, 0, where)
                values = geo.keys_of(own, own_r, slot, 1, where)
                query, grad = queries[slot, 0], queries[slot, 1]
                s, dp = geo.scores(keys, values, query, grad, where)
                top, inverse, delta = get_stats(stats, pair, side)
                ok = on & geo.has(geo.frame + step)
                inverse = jnp.where(ok, inverse, jnp.float32(0.0))
                weights, dscores = geo.weigh(jnp.minimum(s, top), dp, top, inverse, delta)
                total[0] = total[0] + geo.fold(dot_nn(dscores, query), where)
                total[1] = total[1] + geo.fold(dot_nn(weights, grad), where)
            cols = columns(head, dim)
            for j in range(2):
                grads[slot, j] = total[j][width : width + tokens].astype(BF16)
                rim_low[j, :, cols] = total[j][:width].astype(BF16)
                rim_high[j, :, cols] = total[j][width + tokens :].astype(BF16)
        return carry

    lax.fori_loop(0, n // 2, pair_step, 0)
    if others:
        spread_rims(n, order, others[0], rim_low, rim_high, dim)


def spread_rims(n, order, rims, rim_low, rim_high, dim):
    def put(i):
        cols = columns(order[n + i], dim)
        for j in range(2):
            rim_low[j, :, cols] = rims[i, 0, j]
            rim_high[j, :, cols] = rims[i, 1, j]

    each(rims.shape[0], put)


def rim_kernel(dim, order, rims, rim_low, rim_high):
    spread_rims(0, order, rims, rim_low, rim_high, dim)


def query_out_kernel(n, dim, order, *refs):
    parts, out = refs[:-1], refs[-1]

    def active(slot):
        out[:, columns(order[slot], dim)] = parts[0][slot]

    def passive(i):
        out[:, columns(order[n + i], dim)] = parts[-1][i, 0]

    if n:
        each(n, active)
    if len(parts) > bool(n):
        each(parts[-1].shape[0], passive)


def last_kernel(n, dim, width, order, below, above, *refs):
    parts, outs = refs[:-2], refs[-2:]
    tokens = outs[0].shape[0]

    def put(j, head, ref, i, at):
        cols = columns(head, dim)
        out = outs[j]
        low = ref[i, at, :width].astype(F32) + below[j, :, cols].astype(F32)
        high = ref[i, at, tokens - width :].astype(F32) + above[j, :, cols].astype(F32)
        out[:width, cols] = low.astype(BF16)
        out[width : tokens - width, cols] = ref[i, at, width : tokens - width]
        out[tokens - width :, cols] = high.astype(BF16)

    def active(slot):
        for j in range(2):
            put(j, order[slot], parts[0], slot, j)

    def passive(i):
        for j in range(2):
            put(j, order[n + i], parts[-1], i, 1 + j)

    if n:
        each(n, active)
    if len(parts) > bool(n):
        each(parts[-1].shape[0], passive)


def call(kernel, ins, outs, flops):
    shapes = [jax.ShapeDtypeStruct(s, d) for s, d in outs]
    moved = sum(x.size * x.dtype.itemsize for x in list(ins) + shapes)
    return pl.pallas_call(
        kernel,
        out_shape=shapes,
        in_specs=[SMEM if x.dtype == jnp.int32 else VMEM for x in ins],
        out_specs=[SMEM if x.dtype == jnp.int32 else VMEM for x in shapes],
        cost_estimate=pl.CostEstimate(flops=flops, bytes_accessed=moved, transcendentals=0),
        compiler_params=pltpu.CompilerParams(vmem_limit_bytes=VMEM_LIMIT),
    )(*ins)


def run(n, *rest):
    return steps(n, *rest)


def steps(n, heads, dim, width, args):
    q, g, k, v, reach, offs = args
    tokens, packed = q.shape
    part = functools.partial
    rim = ((2, width, packed), BF16)
    whole = ((tokens, packed), BF16)
    tile = (tokens, dim)
    longer = (tokens + 2 * width, dim)
    flops = 2 * longer[0] * tokens * dim
    rest = heads - n
    packs = ((n, 2) + tile, BF16)
    order, near, far, *own = call(
        part(first_kernel, n, heads, dim, width), [reach, k, v],
        [((heads,), jnp.int32), rim, rim] + ([packs] if n else []), 0,
    )
    grads_own = rims = None
    if n:
        own = own[0]
        prev, following = both(own)
    near, far = swapped(near, "row", 0), swapped(far, "row", 1)
    if n:
        (own_r,) = call(
            part(rims_kernel, n, dim, width), [order, near, far],
            [((n, 2, 2, width, dim), BF16)], 0,
        )
        prev_r, next_r = both(own_r)
        (own_q,) = call(part(pack_kernel, n, dim), [order, q, g, own_r], [packs], 0)
        q_prev, q_next = both(own_q)
    if rest:
        grads_own, rims = call(
            part(own_kernel, n, heads, dim, width), [order, offs, q, g, k, v, near, far],
            [((rest, 3) + tile, BF16), ((rest, 2, 2, width, dim), BF16)], flops * 5 * rest,
        )
    more = [grads_own] if rest else []
    if n:
        grid = ((n, 3, tokens // 2 + width, tokens), F32)
        stats, s, dp = call(
            part(query_kernel, n, dim, width),
            [order, reach, offs, own_q, own, prev, following, own_r, prev_r, next_r],
            [((n // 2, 8, tokens), F32), grid, grid], flops * 6 * n,
        )
        st_prev, st_next = shifted(stats, "frame", 1), shifted(stats, "frame", -1)
        acc, dq = call(
            part(finish_kernel, n, dim, width),
            [order, reach, offs, own_q, own, prev, following, own_r, prev_r, next_r, stats, s, dp],
            [((n, 2) + longer, F32), ((n,) + tile, BF16)], flops * 5 * n,
        )
        grads, rim_low, rim_high = call(
            part(key_kernel, n, dim, width),
            [order, reach, offs, own, own_r, q_prev, q_next, st_prev, st_next, acc]
            + ([rims] if rest else []),
            [((n, 2) + tile, BF16), rim, rim], flops * 8 * n,
        )
        query_parts, key_parts = [dq] + more, [grads] + more
    else:
        rim_low, rim_high = call(part(rim_kernel, dim), [order, rims], [rim, rim], 0)
        query_parts = key_parts = more
    below, above = shifted(rim_high, "row", 1), shifted(rim_low, "row", -1)
    (dq,) = call(part(query_out_kernel, n, dim), [order] + query_parts, [whole], 0)
    dk, dv = call(
        part(last_kernel, n, dim, width), [order, below, above] + key_parts,
        [whole, whole], 0,
    )
    return dq, dk, dv


def on_device(query_tok, key_tok, value_tok, grad_out, head_reach, tile_offset):
    block = query_tok.shape
    rows_dev, width, packed = block[1:]
    heads = head_reach.shape[0]
    dim = packed // heads
    flat = [x.reshape(rows_dev * width, packed) for x in (query_tok, grad_out, key_tok, value_tok)]
    args = flat + [head_reach, tile_offset]
    count = jnp.sum(head_reach)
    grads = lax.switch(
        sum((count > n).astype(jnp.int32) for n in SIZES[:-1]),
        [functools.partial(run, n, heads, dim, width) for n in SIZES],
        args,
    )
    return tuple(x.reshape(block) for x in grads)


def solution(mesh):
    spec = P("frame", "row", None, None)
    return jax.shard_map(
        on_device,
        mesh=mesh,
        in_specs=(spec, spec, spec, spec, P(), P(None, "row")),
        out_specs=(spec, spec, spec),
        check_vma=False,
    )
```

```python
import functools
import math

import jax
import jax.numpy as jnp
from jax import lax
from jax.experimental import pallas as pl
from jax.experimental.pallas import tpu as pltpu
from jax.sharding import PartitionSpec as P

SIZES = tuple(range(4, 21, 2))
VMEM_LIMIT = 16 << 20
F32, BF16 = jnp.float32, jnp.bfloat16
SMEM = pl.BlockSpec(memory_space=pltpu.SMEM)
VMEM = pl.BlockSpec(memory_space=pltpu.VMEM)


def shifted(block, axis, distance):
    devices = range(lax.axis_size(axis))
    route = [(i - distance, i) for i in devices if i - distance in devices]
    return lax.ppermute(block, axis, route)


def swapped(block, axis, first):
    count = lax.axis_size(axis)
    pairs = [(i, i + 1) for i in range(first, count - 1, 2)]
    return lax.ppermute(block, axis, pairs + [(b, a) for a, b in pairs])


def columns(head, dim):
    return pl.ds(pl.multiple_of(head * dim, dim), dim)


def dot_nt(a, b):
    return lax.dot_general(a, b, (((1,), (1,)), ((), ())), preferred_element_type=F32)


def dot_nn(a, b):
    return lax.dot_general(a, b, (((1,), (0,)), ((), ())), preferred_element_type=F32)


def dot_tn(a, b):
    return lax.dot_general(a, b, (((0,), (0,)), ((), ())), preferred_element_type=F32)


class Geometry:
    def __init__(self, tokens, width, dim):
        self.tokens, self.width, self.dim = tokens, width, dim
        self.half = tokens // 2
        self.scale = 1.0 / math.sqrt(dim)
        self.frames = lax.axis_size("frame")
        self.frame = lax.axis_index("frame")
        self.row = lax.axis_index("row")
        self.rows = lax.axis_size("row")
        self.even = lax.rem(self.row, 2) == 0
        self.low_lanes = lax.broadcasted_iota(jnp.int32, (1, tokens), 1) < self.half

    def has(self, frame):
        return (frame >= 0) & (frame < self.frames)

    def offsets(self, offs_ref, frame):
        frame = jnp.clip(frame, 0, self.frames - 1)
        first, second = offs_ref[frame, 0], offs_ref[frame, 1]
        lost0 = (first == -1) & (self.row == 0)
        lost1 = (second == 0) & (self.row == self.rows - 1)
        fine, gone = jnp.float32(0.0), jnp.float32(-1e30)
        penalty = jnp.where(
            self.low_lanes, jnp.where(lost0, gone, fine), jnp.where(lost1, gone, fine)
        )
        return first == -1, second == -1, penalty

    def rims(self, near, far):
        return jnp.where(self.even, far, near), jnp.where(self.even, near, far)

    def keys(self, main, low, high, offs):
        half, width = self.half, self.width
        edge0 = jnp.where(offs[0], low, main[half : half + width])
        edge1 = jnp.where(offs[1], main[half - width : half], high)
        return jnp.concatenate([main, edge0, edge1], axis=0)

    def keys_of(self, extended, offs):
        width, end = self.width, self.width + self.tokens
        return self.keys(extended[width:end], extended[:width], extended[end:], offs)

    def by_tile(self, product):
        half, width, tokens = self.half, self.width, self.tokens
        own = jnp.where(self.low_lanes, product[:half], product[half:tokens])
        edge = jnp.where(
            self.low_lanes, product[tokens : tokens + width], product[tokens + width :]
        )
        return own, edge

    def scores(self, keys, values, query, grad, offs):
        own, edge = self.by_tile(dot_nt(keys, query))
        s = jnp.concatenate([own * self.scale, edge * self.scale + offs[2]], axis=0)
        dp = jnp.concatenate(self.by_tile(dot_nt(values, grad)), axis=0)
        return s, dp

    def spread(self, terms):
        half = self.half
        own, edge = terms[:half], terms[half:]
        zero_own, zero_edge = jnp.zeros_like(own), jnp.zeros_like(edge)
        low = self.low_lanes
        return jnp.concatenate(
            [
                jnp.where(low, own, zero_own).astype(BF16),
                jnp.where(low, zero_own, own).astype(BF16),
                jnp.where(low, edge, zero_edge).astype(BF16),
                jnp.where(low, zero_edge, edge).astype(BF16),
            ],
            axis=0,
        )

    def weigh(self, s, dp, top, inverse, delta):
        p = jnp.exp(s - top) * inverse
        ds = p * (dp - delta) * self.scale
        return self.spread(p), self.spread(ds)

    def fold(self, term, offs):
        half, width, tokens = self.half, self.width, self.tokens
        edge0, edge1 = term[tokens : tokens + width], term[tokens + width :]
        none = jnp.zeros_like(edge0)
        return jnp.concatenate(
            [
                jnp.where(offs[0], edge0, none),
                term[: half - width],
                term[half - width : half] + jnp.where(offs[1], edge1, none),
                term[half : half + width] + jnp.where(offs[0], none, edge0),
                term[half + width : tokens],
                jnp.where(offs[1], none, edge1),
            ],
            axis=0,
        )


def stats_of(s, dp):
    top = jnp.max(s, axis=0, keepdims=True)
    expo = jnp.exp(s - top)
    return top, jnp.sum(expo, axis=0, keepdims=True), jnp.sum(expo * dp, axis=0, keepdims=True)


def put_stats(ref, pair, side, stats):
    for j, row in enumerate(stats):
        ref[pair, pl.ds(4 * side + j, 1), :] = row


def get_stats(ref, pair, side):
    return [ref[pair, pl.ds(4 * side + j, 1), :] for j in range(3)]


def merge(first, others, valid):
    low = jnp.float32(-1e30)
    tops = [first[0]] + [jnp.where(ok, o[0], low) for o, ok in zip(others, valid)]
    top = functools.reduce(jnp.maximum, tops)
    factor = jnp.exp(first[0] - top)
    total, weighted = first[1] * factor, first[2] * factor
    for o, ok, t in zip(others, valid, tops[1:]):
        factor = jnp.where(ok, jnp.exp(t - top), jnp.float32(0.0))
        total, weighted = total + o[1] * factor, weighted + o[2] * factor
    inverse = 1.0 / total
    return top, inverse, weighted * inverse


def each(count, body):
    def step(i, carry):
        body(i)
        return carry

    lax.fori_loop(0, count, step, 0)


def edge_kernel(heads, reach, k_first, k_last, v_first, v_last, order, near, far):
    even = lax.rem(lax.axis_index("row"), 2) == 0
    for j, (first, last) in enumerate(((k_first, k_last), (v_first, v_last))):
        near[j] = jnp.where(even, last[...], first[...])
        far[j] = jnp.where(even, first[...], last[...])
    count = lax.fori_loop(0, heads, lambda h, c: c + reach[h], 0)

    def place(h, carry):
        on, off = carry
        hit = reach[h] == 1
        order[jnp.where(hit, on, off)] = h
        return jnp.where(hit, on + 1, on), jnp.where(hit, off, off + 1)

    lax.fori_loop(0, heads, place, (0, count))


def edge_rows(k, v, reach, width):
    tokens, packed = k.shape
    first = pl.BlockSpec((width, packed), lambda i: (0, 0))
    last = pl.BlockSpec((width, packed), lambda i: (tokens // width - 1, 0))
    rim = jax.ShapeDtypeStruct((2, width, packed), BF16)
    whole = pl.BlockSpec((2, width, packed), lambda i: (0, 0, 0))
    return pl.pallas_call(
        functools.partial(edge_kernel, reach.shape[0]),
        grid=(1,),
        out_shape=[jax.ShapeDtypeStruct(reach.shape, jnp.int32), rim, rim],
        in_specs=[SMEM, first, last, first, last],
        out_specs=[SMEM, whole, whole],
        compiler_params=pltpu.CompilerParams(vmem_limit_bytes=VMEM_LIMIT),
        name="edge",
    )(reach, k, k, v, v)


def pack_kernel(n, dim, order, q, g, send):
    def pack(slot):
        cols = columns(order[slot], dim)
        send[slot, 0] = q[:, cols]
        send[slot, 1] = g[:, cols]

    each(n, pack)


def extend_kernel(n, dim, width, order, k, v, near, far, send):
    tokens = k.shape[0]
    geo = Geometry(tokens, width, dim)

    def pack(slot):
        cols = columns(order[slot], dim)
        for j, ref in enumerate((k, v)):
            low, high = geo.rims(near[j, :, cols], far[j, :, cols])
            send[slot, j, :width] = low
            send[slot, j, width : width + tokens] = ref[:, cols]
            send[slot, j, width + tokens :] = high

    each(n, pack)


def own_kernel(n, heads, dim, width, order, offs, q, g, k, v, near, far, grads, rims):
    tokens = q.shape[0]
    geo = Geometry(tokens, width, dim)
    where = geo.offsets(offs, geo.frame)

    def finish(pair, carry):
        for side in range(2):
            i = 2 * pair + side
            cols = columns(order[n + i], dim)
            low, high = geo.rims(near[0, :, cols], far[0, :, cols])
            keys = geo.keys(k[:, cols], low, high, where)
            low, high = geo.rims(near[1, :, cols], far[1, :, cols])
            values = geo.keys(v[:, cols], low, high, where)
            query, grad = q[:, cols], g[:, cols]
            s, dp = geo.scores(keys, values, query, grad, where)
            top, total, weighted = stats_of(s, dp)
            inverse = 1.0 / total
            weights, dscores = geo.weigh(s, dp, top, inverse, weighted * inverse)
            grads[i, 0] = dot_tn(dscores, keys).astype(BF16)
            for j, term in enumerate((dot_nn(dscores, query), dot_nn(weights, grad))):
                folded = geo.fold(term, where)
                grads[i, 1 + j] = folded[width : width + tokens].astype(BF16)
                rims[i, 0, j] = folded[:width].astype(BF16)
                rims[i, 1, j] = folded[width + tokens :].astype(BF16)
        return carry

    lax.fori_loop(0, (heads - n) // 2, finish, 0)


def query_kernel(n, dim, width, order, reach, offs, own_q, own, prev, following, stats, s_out, dp_out):
    geo = Geometry(own_q.shape[2], width, dim)
    where = geo.offsets(offs, geo.frame)
    has_prev, has_next = geo.has(geo.frame - 1), geo.has(geo.frame + 1)

    def pair_step(pair, carry):
        for side in range(2):
            slot = 2 * pair + side
            on = reach[order[slot]] == 1
            parts = []
            for i, block in enumerate((own, prev, following)):
                keys = geo.keys_of(block[slot, 0], where)
                values = geo.keys_of(block[slot, 1], where)
                s, dp = geo.scores(keys, values, own_q[slot, 0], own_q[slot, 1], where)
                s_out[slot, i] = s
                dp_out[slot, i] = dp
                parts.append(stats_of(s, dp))
            put_stats(stats, pair, side, merge(parts[0], parts[1:], [on & has_prev, on & has_next]))
        return carry

    lax.fori_loop(0, n // 2, pair_step, 0)


def finish_kernel(
    n, dim, width, order, reach, offs, own_q, own, prev, following, stats, s_in, dp_in, acc, dq
):
    geo = Geometry(own_q.shape[2], width, dim)
    where = geo.offsets(offs, geo.frame)
    has_prev, has_next = geo.has(geo.frame - 1), geo.has(geo.frame + 1)

    def pair_step(pair, carry):
        for side in range(2):
            slot = 2 * pair + side
            on = reach[order[slot]] == 1
            top, inverse, delta = get_stats(stats, pair, side)
            total = None
            for i, (block, ok) in enumerate(
                ((own, None), (prev, on & has_prev), (following, on & has_next))
            ):
                keys = geo.keys_of(block[slot, 0], where)
                part = inverse if ok is None else jnp.where(ok, inverse, jnp.float32(0.0))
                s = s_in[slot, i] if ok is None else jnp.minimum(s_in[slot, i], top)
                weights, dscores = geo.weigh(s, dp_in[slot, i], top, part, delta)
                term = dot_tn(dscores, keys)
                total = term if total is None else total + term
                if ok is None:
                    acc[slot, 0] = geo.fold(dot_nn(dscores, own_q[slot, 0]), where)
                    acc[slot, 1] = geo.fold(dot_nn(weights, own_q[slot, 1]), where)
            dq[slot] = total.astype(BF16)
        return carry

    lax.fori_loop(0, n // 2, pair_step, 0)


def key_kernel(
    n, dim, width, order, reach, offs, own, q_prev, q_next, st_prev, st_next, acc, *refs
):
    tokens = q_prev.shape[2]
    geo = Geometry(tokens, width, dim)
    others, (grads, rim_low, rim_high) = refs[:-3], refs[-3:]

    def pair_step(pair, carry):
        for side in range(2):
            slot = 2 * pair + side
            head = order[slot]
            on = reach[head] == 1
            total = [acc[slot, 0], acc[slot, 1]]
            for step, queries, stats in ((-1, q_prev, st_prev), (1, q_next, st_next)):
                where = geo.offsets(offs, geo.frame + step)
                keys = geo.keys_of(own[slot, 0], where)
                values = geo.keys_of(own[slot, 1], where)
                query, grad = queries[slot, 0], queries[slot, 1]
                s, dp = geo.scores(keys, values, query, grad, where)
                top, inverse, delta = get_stats(stats, pair, side)
                ok = on & geo.has(geo.frame + step)
                inverse = jnp.where(ok, inverse, jnp.float32(0.0))
                weights, dscores = geo.weigh(jnp.minimum(s, top), dp, top, inverse, delta)
                total[0] = total[0] + geo.fold(dot_nn(dscores, query), where)
                total[1] = total[1] + geo.fold(dot_nn(weights, grad), where)
            cols = columns(head, dim)
            for j in range(2):
                grads[slot, j] = total[j][width : width + tokens].astype(BF16)
                rim_low[j, :, cols] = total[j][:width].astype(BF16)
                rim_high[j, :, cols] = total[j][width + tokens :].astype(BF16)
        return carry

    lax.fori_loop(0, n // 2, pair_step, 0)
    if others:
        spread_rims(n, order, others[0], rim_low, rim_high, dim)


def spread_rims(n, order, rims, rim_low, rim_high, dim):
    def put(i):
        cols = columns(order[n + i], dim)
        for j in range(2):
            rim_low[j, :, cols] = rims[i, 0, j]
            rim_high[j, :, cols] = rims[i, 1, j]

    each(rims.shape[0], put)


def query_out_kernel(n, dim, order, *refs):
    parts, out = refs[:-1], refs[-1]

    def active(slot):
        out[:, columns(order[slot], dim)] = parts[0][slot]

    def passive(i):
        out[:, columns(order[n + i], dim)] = parts[1][i, 0]

    each(n, active)
    if len(parts) > 1:
        each(parts[1].shape[0], passive)


def last_kernel(n, dim, width, order, below, above, *refs):
    parts, outs = refs[:-2], refs[-2:]
    tokens = outs[0].shape[0]

    def put(j, head, ref, i, at):
        cols = columns(head, dim)
        out = outs[j]
        low = ref[i, at, :width].astype(F32) + below[j, :, cols].astype(F32)
        high = ref[i, at, tokens - width :].astype(F32) + above[j, :, cols].astype(F32)
        out[:width, cols] = low.astype(BF16)
        out[width : tokens - width, cols] = ref[i, at, width : tokens - width]
        out[tokens - width :, cols] = high.astype(BF16)

    def active(slot):
        for j in range(2):
            put(j, order[slot], parts[0], slot, j)

    def passive(i):
        for j in range(2):
            put(j, order[n + i], parts[1], i, 1 + j)

    each(n, active)
    if len(parts) > 1:
        each(parts[1].shape[0], passive)


def call(name, kernel, ins, outs, flops):
    shapes = [jax.ShapeDtypeStruct(s, d) for s, d in outs]
    moved = sum(x.size * x.dtype.itemsize for x in list(ins) + shapes)
    return pl.pallas_call(
        kernel,
        out_shape=shapes,
        in_specs=[SMEM if x.dtype == jnp.int32 else VMEM for x in ins],
        out_specs=[SMEM if x.dtype == jnp.int32 else VMEM for x in shapes],
        cost_estimate=pl.CostEstimate(flops=flops, bytes_accessed=moved, transcendentals=0),
        compiler_params=pltpu.CompilerParams(vmem_limit_bytes=VMEM_LIMIT),
        name=name,
    )(*ins)


def run(n, heads, dim, width, args):
    q, g, k, v, reach, offs, order, near, far = args
    tokens, packed = q.shape
    part = functools.partial
    rim = ((2, width, packed), BF16)
    whole = ((tokens, packed), BF16)
    tile = (tokens, dim)
    longer = (tokens + 2 * width, dim)
    flops = 2 * longer[0] * tokens * dim
    rest = heads - n
    (own,) = call(
        "extend", part(extend_kernel, n, dim, width), [order, k, v, near, far],
        [((n, 2) + longer, BF16)], 0,
    )
    prev, following = shifted(own, "frame", 1), shifted(own, "frame", -1)
    (own_q,) = call("pack", part(pack_kernel, n, dim), [order, q, g], [((n, 2) + tile, BF16)], 0)
    q_prev, q_next = shifted(own_q, "frame", 1), shifted(own_q, "frame", -1)
    more, rims = [], []
    if rest:
        grads_own, rims_own = call(
            "own", part(own_kernel, n, heads, dim, width), [order, offs, q, g, k, v, near, far],
            [((rest, 3) + tile, BF16), ((rest, 2, 2, width, dim), BF16)], flops * 5 * rest,
        )
        more, rims = [grads_own], [rims_own]
    grid = ((n, 3, tokens // 2 + width, tokens), F32)
    stats, s, dp = call(
        "query", part(query_kernel, n, dim, width),
        [order, reach, offs, own_q, own, prev, following],
        [((n // 2, 8, tokens), F32), grid, grid], flops * 6 * n,
    )
    st_prev, st_next = shifted(stats, "frame", 1), shifted(stats, "frame", -1)
    acc, dq = call(
        "finish", part(finish_kernel, n, dim, width),
        [order, reach, offs, own_q, own, prev, following, stats, s, dp],
        [((n, 2) + longer, F32), ((n,) + tile, BF16)], flops * 5 * n,
    )
    grads, rim_low, rim_high = call(
        "key", part(key_kernel, n, dim, width),
        [order, reach, offs, own, q_prev, q_next, st_prev, st_next, acc] + rims,
        [((n, 2) + tile, BF16), rim, rim], flops * 8 * n,
    )
    below, above = shifted(rim_high, "row", 1), shifted(rim_low, "row", -1)
    (dq,) = call("dq", part(query_out_kernel, n, dim), [order, dq] + more, [whole], 0)
    dk, dv = call(
        "last", part(last_kernel, n, dim, width), [order, below, above, grads] + more,
        [whole, whole], 0,
    )
    return dq, dk, dv


def on_device(query_tok, key_tok, value_tok, grad_out, head_reach, tile_offset):
    block = query_tok.shape
    rows_dev, width, packed = block[1:]
    heads = head_reach.shape[0]
    dim = packed // heads
    flat = [x.reshape(rows_dev * width, packed) for x in (query_tok, grad_out, key_tok, value_tok)]
    order, near, far = edge_rows(flat[2], flat[3], head_reach, width)
    near, far = swapped(near, "row", 0), swapped(far, "row", 1)
    args = flat + [head_reach, tile_offset, order, near, far]
    sizes = [min(n, heads) for n in SIZES]
    count = jnp.sum(head_reach)
    grads = lax.switch(
        lax.shift_right_arithmetic(count - (SIZES[0] - 1), 1),
        [functools.partial(run, n, heads, dim, width) for n in sizes],
        args,
    )
    return tuple(x.reshape(block) for x in grads)


def solution(mesh):
    spec = P("frame", "row", None, None)
    return jax.shard_map(
        on_device,
        mesh=mesh,
        in_specs=(spec, spec, spec, spec, P(), P(None, "row")),
        out_specs=(spec, spec, spec),
        check_vma=False,
    )
```

```python
import functools
import math

import jax
import jax.numpy as jnp
from jax import lax
from jax.experimental import pallas as pl
from jax.experimental.pallas import tpu as pltpu
from jax.sharding import PartitionSpec as P

SIZES = (6, 8, 10, 12, 14, 16, 20)
VMEM_LIMIT = 16 << 20
F32, BF16 = jnp.float32, jnp.bfloat16
SMEM = pl.BlockSpec(memory_space=pltpu.SMEM)
VMEM = pl.BlockSpec(memory_space=pltpu.VMEM)


def shifted(block, axis, distance):
    devices = range(lax.axis_size(axis))
    route = [(i - distance, i) for i in devices if i - distance in devices]
    return lax.ppermute(block, axis, route)


def swapped(block, axis, first):
    count = lax.axis_size(axis)
    pairs = [(i, i + 1) for i in range(first, count - 1, 2)]
    return lax.ppermute(block, axis, pairs + [(b, a) for a, b in pairs])


def columns(head, dim):
    return pl.ds(pl.multiple_of(head * dim, dim), dim)


def dot_nt(a, b):
    return lax.dot_general(a, b, (((1,), (1,)), ((), ())), preferred_element_type=F32)


def dot_nn(a, b):
    return lax.dot_general(a, b, (((1,), (0,)), ((), ())), preferred_element_type=F32)


def dot_tn(a, b):
    return lax.dot_general(a, b, (((0,), (0,)), ((), ())), preferred_element_type=F32)


class Geometry:
    def __init__(self, tokens, width, dim):
        self.tokens, self.width, self.dim = tokens, width, dim
        self.half = tokens // 2
        self.scale = 1.0 / math.sqrt(dim)
        self.frames = lax.axis_size("frame")
        self.frame = lax.axis_index("frame")
        self.row = lax.axis_index("row")
        self.rows = lax.axis_size("row")
        self.even = lax.rem(self.row, 2) == 0
        self.low_lanes = lax.broadcasted_iota(jnp.int32, (1, tokens), 1) < self.half

    def has(self, frame):
        return (frame >= 0) & (frame < self.frames)

    def offsets(self, offs_ref, frame):
        frame = jnp.clip(frame, 0, self.frames - 1)
        first, second = offs_ref[frame, 0], offs_ref[frame, 1]
        lost0 = (first == -1) & (self.row == 0)
        lost1 = (second == 0) & (self.row == self.rows - 1)
        fine, gone = jnp.float32(0.0), jnp.float32(-1e30)
        penalty = jnp.where(
            self.low_lanes, jnp.where(lost0, gone, fine), jnp.where(lost1, gone, fine)
        )
        return first == -1, second == -1, penalty

    def rims(self, near, far):
        return jnp.where(self.even, far, near), jnp.where(self.even, near, far)

    def keys(self, main, low, high, offs):
        half, width = self.half, self.width
        edge0 = jnp.where(offs[0], low, main[half : half + width])
        edge1 = jnp.where(offs[1], main[half - width : half], high)
        return jnp.concatenate([main, edge0, edge1], axis=0)

    def keys_of(self, extended, offs):
        width, end = self.width, self.width + self.tokens
        return self.keys(extended[width:end], extended[:width], extended[end:], offs)

    def by_tile(self, product):
        half, width, tokens = self.half, self.width, self.tokens
        own = jnp.where(self.low_lanes, product[:half], product[half:tokens])
        edge = jnp.where(
            self.low_lanes, product[tokens : tokens + width], product[tokens + width :]
        )
        return own, edge

    def scores(self, keys, values, query, grad, offs):
        own, edge = self.by_tile(dot_nt(keys, query))
        s = jnp.concatenate([own * self.scale, edge * self.scale + offs[2]], axis=0)
        dp = jnp.concatenate(self.by_tile(dot_nt(values, grad)), axis=0)
        return s, dp

    def spread(self, terms):
        half = self.half
        own, edge = terms[:half], terms[half:]
        zero_own, zero_edge = jnp.zeros_like(own), jnp.zeros_like(edge)
        low = self.low_lanes
        return jnp.concatenate(
            [
                jnp.where(low, own, zero_own).astype(BF16),
                jnp.where(low, zero_own, own).astype(BF16),
                jnp.where(low, edge, zero_edge).astype(BF16),
                jnp.where(low, zero_edge, edge).astype(BF16),
            ],
            axis=0,
        )

    def weigh(self, s, dp, top, inverse, delta):
        p = jnp.exp(s - top) * inverse
        ds = p * (dp - delta) * self.scale
        return self.spread(p), self.spread(ds)

    def fold(self, term, offs):
        half, width, tokens = self.half, self.width, self.tokens
        edge0, edge1 = term[tokens : tokens + width], term[tokens + width :]
        none = jnp.zeros_like(edge0)
        return jnp.concatenate(
            [
                jnp.where(offs[0], edge0, none),
                term[: half - width],
                term[half - width : half] + jnp.where(offs[1], edge1, none),
                term[half : half + width] + jnp.where(offs[0], none, edge0),
                term[half + width : tokens],
                jnp.where(offs[1], none, edge1),
            ],
            axis=0,
        )


def stats_of(s, dp):
    top = jnp.max(s, axis=0, keepdims=True)
    expo = jnp.exp(s - top)
    return top, jnp.sum(expo, axis=0, keepdims=True), jnp.sum(expo * dp, axis=0, keepdims=True)


def put_stats(ref, pair, side, stats):
    for j, row in enumerate(stats):
        ref[pair, pl.ds(4 * side + j, 1), :] = row


def get_stats(ref, pair, side):
    return [ref[pair, pl.ds(4 * side + j, 1), :] for j in range(3)]


def merge(first, others, valid):
    low = jnp.float32(-1e30)
    tops = [first[0]] + [jnp.where(ok, o[0], low) for o, ok in zip(others, valid)]
    top = functools.reduce(jnp.maximum, tops)
    factor = jnp.exp(first[0] - top)
    total, weighted = first[1] * factor, first[2] * factor
    for o, ok, t in zip(others, valid, tops[1:]):
        factor = jnp.where(ok, jnp.exp(t - top), jnp.float32(0.0))
        total, weighted = total + o[1] * factor, weighted + o[2] * factor
    inverse = 1.0 / total
    return top, inverse, weighted * inverse


def each(count, body):
    def step(i, carry):
        body(i)
        return carry

    lax.fori_loop(0, count, step, 0)


def edge_kernel(heads, reach, k_first, k_last, v_first, v_last, order, near, far):
    even = lax.rem(lax.axis_index("row"), 2) == 0
    for j, (first, last) in enumerate(((k_first, k_last), (v_first, v_last))):
        near[j] = jnp.where(even, last[...], first[...])
        far[j] = jnp.where(even, first[...], last[...])
    count = lax.fori_loop(0, heads, lambda h, c: c + reach[h], 0)

    def place(h, carry):
        on, off = carry
        hit = reach[h] == 1
        order[jnp.where(hit, on, off)] = h
        return jnp.where(hit, on + 1, on), jnp.where(hit, off, off + 1)

    lax.fori_loop(0, heads, place, (0, count))


def edge_rows(k, v, reach, width):
    tokens, packed = k.shape
    first = pl.BlockSpec((width, packed), lambda i: (0, 0))
    last = pl.BlockSpec((width, packed), lambda i: (tokens // width - 1, 0))
    rim = jax.ShapeDtypeStruct((2, width, packed), BF16)
    whole = pl.BlockSpec((2, width, packed), lambda i: (0, 0, 0))
    return pl.pallas_call(
        functools.partial(edge_kernel, reach.shape[0]),
        grid=(1,),
        out_shape=[jax.ShapeDtypeStruct(reach.shape, jnp.int32), rim, rim],
        in_specs=[SMEM, first, last, first, last],
        out_specs=[SMEM, whole, whole],
        compiler_params=pltpu.CompilerParams(vmem_limit_bytes=VMEM_LIMIT),
        name="edge",
    )(reach, k, k, v, v)


def pack_kernel(n, dim, order, q, g, send):
    def pack(slot):
        cols = columns(order[slot], dim)
        send[slot, 0] = q[:, cols]
        send[slot, 1] = g[:, cols]

    each(n, pack)


def extend_kernel(n, dim, width, order, k, v, near, far, send):
    tokens = k.shape[0]
    geo = Geometry(tokens, width, dim)

    for slot in range(n):
        cols = columns(order[slot], dim)
        for j, ref in enumerate((k, v)):
            low, high = geo.rims(near[j, :, cols], far[j, :, cols])
            send[slot, j, :width] = low
            send[slot, j, width : width + tokens] = ref[:, cols]
            send[slot, j, width + tokens :] = high


def own_kernel(n, heads, dim, width, order, offs, q, g, k, v, near, far, grads, rims):
    tokens = q.shape[0]
    geo = Geometry(tokens, width, dim)
    where = geo.offsets(offs, geo.frame)

    def finish(i):
        cols = columns(order[n + i], dim)
        low, high = geo.rims(near[0, :, cols], far[0, :, cols])
        keys = geo.keys(k[:, cols], low, high, where)
        low, high = geo.rims(near[1, :, cols], far[1, :, cols])
        values = geo.keys(v[:, cols], low, high, where)
        query, grad = q[:, cols], g[:, cols]
        s, dp = geo.scores(keys, values, query, grad, where)
        top, total, weighted = stats_of(s, dp)
        inverse = 1.0 / total
        weights, dscores = geo.weigh(s, dp, top, inverse, weighted * inverse)
        grads[i, 0] = dot_tn(dscores, keys).astype(BF16)
        for j, term in enumerate((dot_nn(dscores, query), dot_nn(weights, grad))):
            folded = geo.fold(term, where)
            grads[i, 1 + j] = folded[width : width + tokens].astype(BF16)
            rims[i, 0, j] = folded[:width].astype(BF16)
            rims[i, 1, j] = folded[width + tokens :].astype(BF16)

    each(heads - n, finish)


def query_kernel(n, dim, width, order, reach, offs, own_q, own, prev, following, stats, s_out, dp_out):
    geo = Geometry(own_q.shape[2], width, dim)
    where = geo.offsets(offs, geo.frame)
    has_prev, has_next = geo.has(geo.frame - 1), geo.has(geo.frame + 1)

    def pair_step(pair, carry):
        for side in range(2):
            slot = 2 * pair + side
            on = reach[order[slot]] == 1
            parts = []
            for i, block in enumerate((own, prev, following)):
                keys = geo.keys_of(block[slot, 0], where)
                values = geo.keys_of(block[slot, 1], where)
                s, dp = geo.scores(keys, values, own_q[slot, 0], own_q[slot, 1], where)
                s_out[slot, i] = s
                dp_out[slot, i] = dp
                parts.append(stats_of(s, dp))
            put_stats(stats, pair, side, merge(parts[0], parts[1:], [on & has_prev, on & has_next]))
        return carry

    lax.fori_loop(0, n // 2, pair_step, 0)


def finish_kernel(
    n, dim, width, order, reach, offs, own_q, own, prev, following, stats, s_in, dp_in, acc, dq
):
    geo = Geometry(own_q.shape[2], width, dim)
    where = geo.offsets(offs, geo.frame)
    has_prev, has_next = geo.has(geo.frame - 1), geo.has(geo.frame + 1)

    def pair_step(pair, carry):
        for side in range(2):
            slot = 2 * pair + side
            on = reach[order[slot]] == 1
            top, inverse, delta = get_stats(stats, pair, side)
            total = None
            for i, (block, ok) in enumerate(
                ((own, None), (prev, on & has_prev), (following, on & has_next))
            ):
                keys = geo.keys_of(block[slot, 0], where)
                part = inverse if ok is None else jnp.where(ok, inverse, jnp.float32(0.0))
                s = s_in[slot, i] if ok is None else jnp.minimum(s_in[slot, i], top)
                weights, dscores = geo.weigh(s, dp_in[slot, i], top, part, delta)
                term = dot_tn(dscores, keys)
                total = term if total is None else total + term
                if ok is None:
                    acc[slot, 0] = geo.fold(dot_nn(dscores, own_q[slot, 0]), where)
                    acc[slot, 1] = geo.fold(dot_nn(weights, own_q[slot, 1]), where)
            dq[slot] = total.astype(BF16)
        return carry

    lax.fori_loop(0, n // 2, pair_step, 0)


def weigh_kernel(
    n, dim, width, order, reach, offs, own, q_prev, q_next, st_prev, st_next, acc, *refs
):
    tokens = q_prev.shape[2]
    geo = Geometry(tokens, width, dim)
    others, (kept, rim_low, rim_high) = refs[:-3], refs[-3:]

    def pair_step(pair):
        for side in range(2):
            slot = 2 * pair + side
            head = order[slot]
            on = reach[head] == 1
            lows = [acc[slot, j, :width] for j in range(2)]
            highs = [acc[slot, j, width + tokens :] for j in range(2)]
            for i, (step, queries, stats) in enumerate(
                ((-1, q_prev, st_prev), (1, q_next, st_next))
            ):
                where = geo.offsets(offs, geo.frame + step)
                keys = geo.keys_of(own[slot, 0], where)
                values = geo.keys_of(own[slot, 1], where)
                sources = queries[slot, 0], queries[slot, 1]
                s, dp = geo.scores(keys, values, *sources, where)
                top, inverse, delta = get_stats(stats, pair, side)
                ok = on & geo.has(geo.frame + step)
                inverse = jnp.where(ok, inverse, jnp.float32(0.0))
                weights, dscores = geo.weigh(jnp.minimum(s, top), dp, top, inverse, delta)
                for j, part in enumerate((dscores, weights)):
                    kept[slot, i, j] = part
                    edges = dot_nn(part[tokens:], sources[j])
                    none = jnp.zeros_like(lows[j])
                    lows[j] = lows[j] + jnp.where(where[0], edges[:width], none)
                    highs[j] = highs[j] + jnp.where(where[1], none, edges[width:])
            cols = columns(head, dim)
            for j in range(2):
                rim_low[j, :, cols] = lows[j].astype(BF16)
                rim_high[j, :, cols] = highs[j].astype(BF16)

    each(n // 2, pair_step)
    if others:
        spread_rims(n, order, others[0], rim_low, rim_high, dim)


def key_kernel(n, dim, width, offs, q_prev, q_next, kept, acc, grads):
    tokens = q_prev.shape[2]
    geo = Geometry(tokens, width, dim)
    places = [geo.offsets(offs, geo.frame + step) for step in (-1, 1)]

    def pair_step(pair):
        for side in range(2):
            slot = 2 * pair + side
            for j in range(2):
                total = acc[slot, j, width : width + tokens]
                for i, queries in enumerate((q_prev, q_next)):
                    folded = geo.fold(dot_nn(kept[slot, i, j], queries[slot, j]), places[i])
                    total = total + folded[width : width + tokens]
                grads[slot, j] = total.astype(BF16)

    each(n // 2, pair_step)


def spread_rims(n, order, rims, rim_low, rim_high, dim):
    def put(i):
        cols = columns(order[n + i], dim)
        for j in range(2):
            rim_low[j, :, cols] = rims[i, 0, j]
            rim_high[j, :, cols] = rims[i, 1, j]

    each(rims.shape[0], put)


def query_out_kernel(n, dim, order, *refs):
    parts, out = refs[:-1], refs[-1]

    def active(slot):
        out[:, columns(order[slot], dim)] = parts[0][slot]

    def passive(i):
        out[:, columns(order[n + i], dim)] = parts[1][i, 0]

    each(n, active)
    if len(parts) > 1:
        each(parts[1].shape[0], passive)


def last_kernel(n, dim, width, order, below, above, *refs):
    parts, outs = refs[:-2], refs[-2:]
    tokens = outs[0].shape[0]

    def put(j, head, ref, i, at):
        cols = columns(head, dim)
        out = outs[j]
        low = ref[i, at, :width].astype(F32) + below[j, :, cols].astype(F32)
        high = ref[i, at, tokens - width :].astype(F32) + above[j, :, cols].astype(F32)
        out[:width, cols] = low.astype(BF16)
        out[width : tokens - width, cols] = ref[i, at, width : tokens - width]
        out[tokens - width :, cols] = high.astype(BF16)

    def active(slot):
        for j in range(2):
            put(j, order[slot], parts[0], slot, j)

    def passive(i):
        for j in range(2):
            put(j, order[n + i], parts[1], i, 1 + j)

    each(n, active)
    if len(parts) > 1:
        each(parts[1].shape[0], passive)


def call(name, kernel, ins, outs, flops):
    shapes = [jax.ShapeDtypeStruct(s, d) for s, d in outs]
    moved = sum(x.size * x.dtype.itemsize for x in list(ins) + shapes)
    return pl.pallas_call(
        kernel,
        out_shape=shapes,
        in_specs=[SMEM if x.dtype == jnp.int32 else VMEM for x in ins],
        out_specs=[SMEM if x.dtype == jnp.int32 else VMEM for x in shapes],
        cost_estimate=pl.CostEstimate(flops=flops, bytes_accessed=moved, transcendentals=0),
        compiler_params=pltpu.CompilerParams(vmem_limit_bytes=VMEM_LIMIT),
        name=name,
    )(*ins)


def run(n, heads, dim, width, args):
    q, g, k, v, reach, offs, order, near, far = args
    tokens, packed = q.shape
    part = functools.partial
    rim = ((2, width, packed), BF16)
    whole = ((tokens, packed), BF16)
    tile = (tokens, dim)
    longer = (tokens + 2 * width, dim)
    flops = 2 * longer[0] * tokens * dim
    rest = heads - n
    (own,) = call(
        "extend", part(extend_kernel, n, dim, width), [order, k, v, near, far],
        [((n, 2) + longer, BF16)], 0,
    )
    prev, following = shifted(own, "frame", 1), shifted(own, "frame", -1)
    (own_q,) = call("pack", part(pack_kernel, n, dim), [order, q, g], [((n, 2) + tile, BF16)], 0)
    q_prev, q_next = shifted(own_q, "frame", 1), shifted(own_q, "frame", -1)
    more, rims = [], []
    if rest:
        grads_own, rims_own = call(
            "own", part(own_kernel, n, heads, dim, width), [order, offs, q, g, k, v, near, far],
            [((rest, 3) + tile, BF16), ((rest, 2, 2, width, dim), BF16)], flops * 5 * rest,
        )
        more, rims = [grads_own], [rims_own]
    grid = ((n, 3, tokens // 2 + width, tokens), F32)
    stats, s, dp = call(
        "query", part(query_kernel, n, dim, width),
        [order, reach, offs, own_q, own, prev, following],
        [((n // 2, 8, tokens), F32), grid, grid], flops * 6 * n,
    )
    st_prev, st_next = shifted(stats, "frame", 1), shifted(stats, "frame", -1)
    acc, dq = call(
        "finish", part(finish_kernel, n, dim, width),
        [order, reach, offs, own_q, own, prev, following, stats, s, dp],
        [((n, 2) + longer, F32), ((n,) + tile, BF16)], flops * 5 * n,
    )
    kept, rim_low, rim_high = call(
        "weigh", part(weigh_kernel, n, dim, width),
        [order, reach, offs, own, q_prev, q_next, st_prev, st_next, acc] + rims,
        [((n, 2, 2) + longer, BF16), rim, rim], flops * 5 * n,
    )
    below, above = shifted(rim_high, "row", 1), shifted(rim_low, "row", -1)
    (grads,) = call(
        "key", part(key_kernel, n, dim, width), [offs, q_prev, q_next, kept, acc],
        [((n, 2) + tile, BF16)], flops * 4 * n,
    )
    (dq,) = call("dq", part(query_out_kernel, n, dim), [order, dq] + more, [whole], 0)
    dk, dv = call(
        "last", part(last_kernel, n, dim, width), [order, below, above, grads] + more,
        [whole, whole], 0,
    )
    return dq, dk, dv


def on_device(query_tok, key_tok, value_tok, grad_out, head_reach, tile_offset):
    block = query_tok.shape
    rows_dev, width, packed = block[1:]
    heads = head_reach.shape[0]
    dim = packed // heads
    flat = [x.reshape(rows_dev * width, packed) for x in (query_tok, grad_out, key_tok, value_tok)]
    order, near, far = edge_rows(flat[2], flat[3], head_reach, width)
    near, far = swapped(near, "row", 0), swapped(far, "row", 1)
    args = flat + [head_reach, tile_offset, order, near, far]
    sizes = [min(n, heads) for n in SIZES]
    count = jnp.sum(head_reach)
    grads = lax.switch(
        lax.shift_right_arithmetic(count - (SIZES[0] - 1), 1),
        [functools.partial(run, n, heads, dim, width) for n in sizes],
        args,
    )
    return tuple(x.reshape(block) for x in grads)


def solution(mesh):
    spec = P("frame", "row", None, None)
    return jax.shard_map(
        on_device,
        mesh=mesh,
        in_specs=(spec, spec, spec, spec, P(), P(None, "row")),
        out_specs=(spec, spec, spec),
        check_vma=False,
    )
```

```python
import functools
import math

import jax
import jax.numpy as jnp
from jax import lax
from jax.experimental import pallas as pl
from jax.experimental.pallas import tpu as pltpu
from jax.sharding import PartitionSpec as P

SIZES = (6, 8, 10, 12, 14, 16, 20)
VMEM_LIMIT = 16 << 20
F32, BF16 = jnp.float32, jnp.bfloat16
SMEM = pl.BlockSpec(memory_space=pltpu.SMEM)
VMEM = pl.BlockSpec(memory_space=pltpu.VMEM)


def shifted(block, axis, distance):
    devices = range(lax.axis_size(axis))
    route = [(i - distance, i) for i in devices if i - distance in devices]
    return lax.ppermute(block, axis, route)


def swapped(block, axis, first):
    count = lax.axis_size(axis)
    pairs = [(i, i + 1) for i in range(first, count - 1, 2)]
    return lax.ppermute(block, axis, pairs + [(b, a) for a, b in pairs])


def columns(head, dim):
    return pl.ds(pl.multiple_of(head * dim, dim), dim)


def dot_nt(a, b):
    return lax.dot_general(a, b, (((1,), (1,)), ((), ())), preferred_element_type=F32)


def dot_nn(a, b):
    return lax.dot_general(a, b, (((1,), (0,)), ((), ())), preferred_element_type=F32)


def dot_tn(a, b):
    return lax.dot_general(a, b, (((0,), (0,)), ((), ())), preferred_element_type=F32)


class Geometry:
    def __init__(self, tokens, width, dim):
        self.tokens, self.width, self.dim = tokens, width, dim
        self.half = tokens // 2
        self.scale = 1.0 / math.sqrt(dim)
        self.frames = lax.axis_size("frame")
        self.frame = lax.axis_index("frame")
        self.row = lax.axis_index("row")
        self.rows = lax.axis_size("row")
        self.even = lax.rem(self.row, 2) == 0
        self.low_lanes = lax.broadcasted_iota(jnp.int32, (1, tokens), 1) < self.half

    def has(self, frame):
        return (frame >= 0) & (frame < self.frames)

    def offsets(self, offs_ref, frame):
        frame = jnp.clip(frame, 0, self.frames - 1)
        first, second = offs_ref[frame, 0], offs_ref[frame, 1]
        lost0 = (first == -1) & (self.row == 0)
        lost1 = (second == 0) & (self.row == self.rows - 1)
        fine, gone = jnp.float32(0.0), jnp.float32(-1e30)
        penalty = jnp.where(
            self.low_lanes, jnp.where(lost0, gone, fine), jnp.where(lost1, gone, fine)
        )
        return first == -1, second == -1, penalty

    def rims(self, near, far):
        return jnp.where(self.even, far, near), jnp.where(self.even, near, far)

    def keys(self, main, low, high, offs):
        half, width = self.half, self.width
        edge0 = jnp.where(offs[0], low, main[half : half + width])
        edge1 = jnp.where(offs[1], main[half - width : half], high)
        return jnp.concatenate([main, edge0, edge1], axis=0)

    def keys_of(self, extended, offs):
        width, end = self.width, self.width + self.tokens
        return self.keys(extended[width:end], extended[:width], extended[end:], offs)

    def by_tile(self, product):
        half, width, tokens = self.half, self.width, self.tokens
        own = jnp.where(self.low_lanes, product[:half], product[half:tokens])
        edge = jnp.where(
            self.low_lanes, product[tokens : tokens + width], product[tokens + width :]
        )
        return own, edge

    def scores(self, keys, values, query, grad, offs):
        own, edge = self.by_tile(dot_nt(keys, query))
        s = jnp.concatenate([own * self.scale, edge * self.scale + offs[2]], axis=0)
        dp = jnp.concatenate(self.by_tile(dot_nt(values, grad)), axis=0)
        return s, dp

    def spread(self, terms):
        half = self.half
        own, edge = terms[:half], terms[half:]
        zero_own, zero_edge = jnp.zeros_like(own), jnp.zeros_like(edge)
        low = self.low_lanes
        return jnp.concatenate(
            [
                jnp.where(low, own, zero_own).astype(BF16),
                jnp.where(low, zero_own, own).astype(BF16),
                jnp.where(low, edge, zero_edge).astype(BF16),
                jnp.where(low, zero_edge, edge).astype(BF16),
            ],
            axis=0,
        )

    def weigh(self, s, dp, top, inverse, delta):
        p = jnp.exp(s - top) * inverse
        ds = p * (dp - delta) * self.scale
        return self.spread(p), self.spread(ds)

    def fold(self, term, offs):
        half, width, tokens = self.half, self.width, self.tokens
        edge0, edge1 = term[tokens : tokens + width], term[tokens + width :]
        none = jnp.zeros_like(edge0)
        return jnp.concatenate(
            [
                jnp.where(offs[0], edge0, none),
                term[: half - width],
                term[half - width : half] + jnp.where(offs[1], edge1, none),
                term[half : half + width] + jnp.where(offs[0], none, edge0),
                term[half + width : tokens],
                jnp.where(offs[1], none, edge1),
            ],
            axis=0,
        )


def stats_of(s, dp):
    top = jnp.max(s, axis=0, keepdims=True)
    expo = jnp.exp(s - top)
    return top, jnp.sum(expo, axis=0, keepdims=True), jnp.sum(expo * dp, axis=0, keepdims=True)


def put_stats(ref, pair, side, stats):
    for j, row in enumerate(stats):
        ref[pair, pl.ds(4 * side + j, 1), :] = row


def get_stats(ref, pair, side):
    return [ref[pair, pl.ds(4 * side + j, 1), :] for j in range(3)]


def merge(first, others, valid):
    low = jnp.float32(-1e30)
    tops = [first[0]] + [jnp.where(ok, o[0], low) for o, ok in zip(others, valid)]
    top = functools.reduce(jnp.maximum, tops)
    factor = jnp.exp(first[0] - top)
    total, weighted = first[1] * factor, first[2] * factor
    for o, ok, t in zip(others, valid, tops[1:]):
        factor = jnp.where(ok, jnp.exp(t - top), jnp.float32(0.0))
        total, weighted = total + o[1] * factor, weighted + o[2] * factor
    inverse = 1.0 / total
    return top, inverse, weighted * inverse


def each(count, body):
    def step(i, carry):
        body(i)
        return carry

    lax.fori_loop(0, count, step, 0)


def edge_kernel(heads, reach, k_first, k_last, v_first, v_last, order, near, far):
    even = lax.rem(lax.axis_index("row"), 2) == 0
    for j, (first, last) in enumerate(((k_first, k_last), (v_first, v_last))):
        near[j] = jnp.where(even, last[...], first[...])
        far[j] = jnp.where(even, first[...], last[...])
    count = lax.fori_loop(0, heads, lambda h, c: c + reach[h], 0)

    def place(h, carry):
        on, off = carry
        hit = reach[h] == 1
        order[jnp.where(hit, on, off)] = h
        return jnp.where(hit, on + 1, on), jnp.where(hit, off, off + 1)

    lax.fori_loop(0, heads, place, (0, count))


def edge_rows(k, v, reach, width):
    tokens, packed = k.shape
    first = pl.BlockSpec((width, packed), lambda i: (0, 0))
    last = pl.BlockSpec((width, packed), lambda i: (tokens // width - 1, 0))
    rim = jax.ShapeDtypeStruct((2, width, packed), BF16)
    whole = pl.BlockSpec((2, width, packed), lambda i: (0, 0, 0))
    return pl.pallas_call(
        functools.partial(edge_kernel, reach.shape[0]),
        grid=(1,),
        out_shape=[jax.ShapeDtypeStruct(reach.shape, jnp.int32), rim, rim],
        in_specs=[SMEM, first, last, first, last],
        out_specs=[SMEM, whole, whole],
        compiler_params=pltpu.CompilerParams(vmem_limit_bytes=VMEM_LIMIT),
        name="edge",
    )(reach, k, k, v, v)


def pack_kernel(n, dim, order, q, g, send):
    def pack(slot):
        cols = columns(order[slot], dim)
        send[slot, 0] = q[:, cols]
        send[slot, 1] = g[:, cols]

    each(n, pack)


def extend_kernel(n, dim, width, order, k, v, near, far, send):
    tokens = k.shape[0]
    geo = Geometry(tokens, width, dim)

    for slot in range(n):
        cols = columns(order[slot], dim)
        for j, ref in enumerate((k, v)):
            low, high = geo.rims(near[j, :, cols], far[j, :, cols])
            send[slot, j, :width] = low
            send[slot, j, width : width + tokens] = ref[:, cols]
            send[slot, j, width + tokens :] = high


def own_kernel(n, heads, dim, width, order, offs, q, g, k, v, near, far, grads, rims):
    tokens = q.shape[0]
    geo = Geometry(tokens, width, dim)
    where = geo.offsets(offs, geo.frame)

    def finish(i):
        cols = columns(order[n + i], dim)
        low, high = geo.rims(near[0, :, cols], far[0, :, cols])
        keys = geo.keys(k[:, cols], low, high, where)
        low, high = geo.rims(near[1, :, cols], far[1, :, cols])
        values = geo.keys(v[:, cols], low, high, where)
        query, grad = q[:, cols], g[:, cols]
        s, dp = geo.scores(keys, values, query, grad, where)
        top, total, weighted = stats_of(s, dp)
        inverse = 1.0 / total
        weights, dscores = geo.weigh(s, dp, top, inverse, weighted * inverse)
        grads[i, 0] = dot_tn(dscores, keys).astype(BF16)
        for j, term in enumerate((dot_nn(dscores, query), dot_nn(weights, grad))):
            folded = geo.fold(term, where)
            grads[i, 1 + j] = folded[width : width + tokens].astype(BF16)
            rims[i, 0, j] = folded[:width].astype(BF16)
            rims[i, 1, j] = folded[width + tokens :].astype(BF16)

    each(heads - n, finish)


def query_kernel(n, dim, width, order, reach, offs, own_q, own, prev, following, stats, s_out, dp_out):
    geo = Geometry(own_q.shape[2], width, dim)
    where = geo.offsets(offs, geo.frame)
    has_prev, has_next = geo.has(geo.frame - 1), geo.has(geo.frame + 1)

    def pair_step(pair, carry):
        for side in range(2):
            slot = 2 * pair + side
            on = reach[order[slot]] == 1
            parts = []
            for i, block in enumerate((own, prev, following)):
                keys = geo.keys_of(block[slot, 0], where)
                values = geo.keys_of(block[slot, 1], where)
                s, dp = geo.scores(keys, values, own_q[slot, 0], own_q[slot, 1], where)
                s_out[slot, i] = s
                dp_out[slot, i] = dp
                parts.append(stats_of(s, dp))
            put_stats(stats, pair, side, merge(parts[0], parts[1:], [on & has_prev, on & has_next]))
        return carry

    lax.fori_loop(0, n // 2, pair_step, 0)


def finish_kernel(
    n, dim, width, order, reach, offs, own_q, own, prev, following, stats, s_in, dp_in, acc, dq
):
    geo = Geometry(own_q.shape[2], width, dim)
    where = geo.offsets(offs, geo.frame)
    has_prev, has_next = geo.has(geo.frame - 1), geo.has(geo.frame + 1)

    def pair_step(pair, carry):
        for side in range(2):
            slot = 2 * pair + side
            on = reach[order[slot]] == 1
            top, inverse, delta = get_stats(stats, pair, side)
            total = None
            for i, (block, ok) in enumerate(
                ((own, None), (prev, on & has_prev), (following, on & has_next))
            ):
                keys = geo.keys_of(block[slot, 0], where)
                part = inverse if ok is None else jnp.where(ok, inverse, jnp.float32(0.0))
                s = s_in[slot, i] if ok is None else jnp.minimum(s_in[slot, i], top)
                weights, dscores = geo.weigh(s, dp_in[slot, i], top, part, delta)
                term = dot_tn(dscores, keys)
                total = term if total is None else total + term
                if ok is None:
                    acc[slot, 0] = geo.fold(dot_nn(dscores, own_q[slot, 0]), where)
                    acc[slot, 1] = geo.fold(dot_nn(weights, own_q[slot, 1]), where)
            dq[slot] = total.astype(BF16)
        return carry

    lax.fori_loop(0, n // 2, pair_step, 0)


def key_kernel(
    n, dim, width, order, reach, offs, own, q_prev, q_next, st_prev, st_next, acc, *refs
):
    tokens = q_prev.shape[2]
    geo = Geometry(tokens, width, dim)
    half, end = tokens // 2, width + tokens
    others, (grads, rim_low, rim_high) = refs[:-3], refs[-3:]
    places = [geo.offsets(offs, geo.frame + step) for step in (-1, 1)]
    penalty = jnp.concatenate([place[2] for place in places], axis=1)
    lane = lax.broadcasted_iota(jnp.int32, (1, 2 * tokens), 1)
    first_tile = lax.rem(lane, tokens) < half
    quarters = [(lane >= i * half) & (lane < (i + 1) * half) for i in range(4)]

    def rows_of(extended):
        main = extended[width:end]
        rows = [main]
        for place in places:
            rows.append(jnp.where(place[0], extended[:width], main[half : half + width]))
            rows.append(jnp.where(place[1], main[half - width : half], extended[end:]))
        return jnp.concatenate(rows, axis=0)

    def by_tile(product):
        main = jnp.where(first_tile, product[:half], product[half:tokens])
        edges = []
        for i in range(2):
            at = tokens + 2 * i * width
            lanes = slice(i * tokens, (i + 1) * tokens)
            edges.append(
                jnp.where(
                    geo.low_lanes,
                    product[at : at + width, lanes],
                    product[at + width : at + 2 * width, lanes],
                )
            )
        return main, jnp.concatenate(edges, axis=1)

    def spread(terms):
        main, edge = terms[:half], terms[half:]
        zero = jnp.zeros_like(main)
        rows = [jnp.where(first_tile, main, zero), jnp.where(first_tile, zero, main)]
        rows += [jnp.where(quarter, edge, jnp.zeros_like(edge)) for quarter in quarters]
        return jnp.concatenate([row.astype(BF16) for row in rows], axis=0)

    def fold(term, base):
        low, main, high = base[:width], base[width:end], base[end:]
        up, down = main[half - width : half], main[half : half + width]
        for i, place in enumerate(places):
            at = tokens + 2 * i * width
            edge0, edge1 = term[at : at + width], term[at + width : at + 2 * width]
            none = jnp.zeros_like(edge0)
            low = low + jnp.where(place[0], edge0, none)
            down = down + jnp.where(place[0], none, edge0)
            up = up + jnp.where(place[1], edge1, none)
            high = high + jnp.where(place[1], none, edge1)
        main = jnp.concatenate([main[: half - width], up, down, main[half + width :]], axis=0)
        return low, main + term[:tokens], high

    def pair_step(pair):
        for side in range(2):
            slot = 2 * pair + side
            head = order[slot]
            on = reach[head] == 1
            query = jnp.concatenate([q_prev[slot, 0], q_next[slot, 0]], axis=0)
            grad = jnp.concatenate([q_prev[slot, 1], q_next[slot, 1]], axis=0)
            main, edge = by_tile(dot_nt(rows_of(own[slot, 0]), query))
            s = jnp.concatenate([main * geo.scale, edge * geo.scale + penalty], axis=0)
            dp = jnp.concatenate(by_tile(dot_nt(rows_of(own[slot, 1]), grad)), axis=0)
            columns_of = []
            for step, stats in ((-1, st_prev), (1, st_next)):
                top, inverse, delta = get_stats(stats, pair, side)
                ok = on & geo.has(geo.frame + step)
                columns_of.append((top, jnp.where(ok, inverse, jnp.float32(0.0)), delta))
            top, inverse, delta = (jnp.concatenate(x, axis=1) for x in zip(*columns_of))
            p = jnp.exp(jnp.minimum(s, top) - top) * inverse
            ds = p * (dp - delta) * geo.scale
            cols = columns(head, dim)
            for j, term in enumerate((dot_nn(spread(ds), query), dot_nn(spread(p), grad))):
                low, main, high = fold(term, acc[slot, j])
                grads[slot, j] = main.astype(BF16)
                rim_low[j, :, cols] = low.astype(BF16)
                rim_high[j, :, cols] = high.astype(BF16)

    each(n // 2, pair_step)
    if others:
        spread_rims(n, order, others[0], rim_low, rim_high, dim)


def spread_rims(n, order, rims, rim_low, rim_high, dim):
    def put(i):
        cols = columns(order[n + i], dim)
        for j in range(2):
            rim_low[j, :, cols] = rims[i, 0, j]
            rim_high[j, :, cols] = rims[i, 1, j]

    each(rims.shape[0], put)


def query_out_kernel(n, dim, order, *refs):
    parts, out = refs[:-1], refs[-1]

    def active(slot):
        out[:, columns(order[slot], dim)] = parts[0][slot]

    def passive(i):
        out[:, columns(order[n + i], dim)] = parts[1][i, 0]

    each(n, active)
    if len(parts) > 1:
        each(parts[1].shape[0], passive)


def last_kernel(n, dim, width, order, below, above, *refs):
    parts, outs = refs[:-2], refs[-2:]
    tokens = outs[0].shape[0]

    def put(j, head, ref, i, at):
        cols = columns(head, dim)
        out = outs[j]
        low = ref[i, at, :width].astype(F32) + below[j, :, cols].astype(F32)
        high = ref[i, at, tokens - width :].astype(F32) + above[j, :, cols].astype(F32)
        out[:width, cols] = low.astype(BF16)
        out[width : tokens - width, cols] = ref[i, at, width : tokens - width]
        out[tokens - width :, cols] = high.astype(BF16)

    def active(slot):
        for j in range(2):
            put(j, order[slot], parts[0], slot, j)

    def passive(i):
        for j in range(2):
            put(j, order[n + i], parts[1], i, 1 + j)

    each(n, active)
    if len(parts) > 1:
        each(parts[1].shape[0], passive)


def call(name, kernel, ins, outs, flops):
    shapes = [jax.ShapeDtypeStruct(s, d) for s, d in outs]
    moved = sum(x.size * x.dtype.itemsize for x in list(ins) + shapes)
    return pl.pallas_call(
        kernel,
        out_shape=shapes,
        in_specs=[SMEM if x.dtype == jnp.int32 else VMEM for x in ins],
        out_specs=[SMEM if x.dtype == jnp.int32 else VMEM for x in shapes],
        cost_estimate=pl.CostEstimate(flops=flops, bytes_accessed=moved, transcendentals=0),
        compiler_params=pltpu.CompilerParams(vmem_limit_bytes=VMEM_LIMIT),
        name=name,
    )(*ins)


def run(n, heads, dim, width, args):
    q, g, k, v, reach, offs, order, near, far = args
    tokens, packed = q.shape
    part = functools.partial
    rim = ((2, width, packed), BF16)
    whole = ((tokens, packed), BF16)
    tile = (tokens, dim)
    longer = (tokens + 2 * width, dim)
    flops = 2 * longer[0] * tokens * dim
    rest = heads - n
    (own,) = call(
        "extend", part(extend_kernel, n, dim, width), [order, k, v, near, far],
        [((n, 2) + longer, BF16)], 0,
    )
    prev, following = shifted(own, "frame", 1), shifted(own, "frame", -1)
    (own_q,) = call("pack", part(pack_kernel, n, dim), [order, q, g], [((n, 2) + tile, BF16)], 0)
    q_prev, q_next = shifted(own_q, "frame", 1), shifted(own_q, "frame", -1)
    more, rims = [], []
    if rest:
        grads_own, rims_own = call(
            "own", part(own_kernel, n, heads, dim, width), [order, offs, q, g, k, v, near, far],
            [((rest, 3) + tile, BF16), ((rest, 2, 2, width, dim), BF16)], flops * 5 * rest,
        )
        more, rims = [grads_own], [rims_own]
    grid = ((n, 3, tokens // 2 + width, tokens), F32)
    stats, s, dp = call(
        "query", part(query_kernel, n, dim, width),
        [order, reach, offs, own_q, own, prev, following],
        [((n // 2, 8, tokens), F32), grid, grid], flops * 6 * n,
    )
    st_prev, st_next = shifted(stats, "frame", 1), shifted(stats, "frame", -1)
    acc, dq = call(
        "finish", part(finish_kernel, n, dim, width),
        [order, reach, offs, own_q, own, prev, following, stats, s, dp],
        [((n, 2) + longer, F32), ((n,) + tile, BF16)], flops * 5 * n,
    )
    grads, rim_low, rim_high = call(
        "key", part(key_kernel, n, dim, width),
        [order, reach, offs, own, q_prev, q_next, st_prev, st_next, acc] + rims,
        [((n, 2) + tile, BF16), rim, rim], flops * 8 * n,
    )
    below, above = shifted(rim_high, "row", 1), shifted(rim_low, "row", -1)
    (dq,) = call("dq", part(query_out_kernel, n, dim), [order, dq] + more, [whole], 0)
    dk, dv = call(
        "last", part(last_kernel, n, dim, width), [order, below, above, grads] + more,
        [whole, whole], 0,
    )
    return dq, dk, dv


def on_device(query_tok, key_tok, value_tok, grad_out, head_reach, tile_offset):
    block = query_tok.shape
    rows_dev, width, packed = block[1:]
    heads = head_reach.shape[0]
    dim = packed // heads
    flat = [x.reshape(rows_dev * width, packed) for x in (query_tok, grad_out, key_tok, value_tok)]
    order, near, far = edge_rows(flat[2], flat[3], head_reach, width)
    near, far = swapped(near, "row", 0), swapped(far, "row", 1)
    args = flat + [head_reach, tile_offset, order, near, far]
    sizes = [min(n, heads) for n in SIZES]
    count = jnp.sum(head_reach)
    grads = lax.switch(
        lax.shift_right_arithmetic(count - (SIZES[0] - 1), 1),
        [functools.partial(run, n, heads, dim, width) for n in sizes],
        args,
    )
    return tuple(x.reshape(block) for x in grads)


def solution(mesh):
    spec = P("frame", "row", None, None)
    return jax.shard_map(
        on_device,
        mesh=mesh,
        in_specs=(spec, spec, spec, spec, P(), P(None, "row")),
        out_specs=(spec, spec, spec),
        check_vma=False,
    )
```

```python
import functools
import math

import jax
import jax.numpy as jnp
from jax import lax
from jax.experimental import pallas as pl
from jax.experimental.pallas import tpu as pltpu
from jax.sharding import PartitionSpec as P

SIZES = (6, 8, 10, 12, 14, 16, 20)
VMEM_LIMIT = 16 << 20
F32, BF16 = jnp.float32, jnp.bfloat16
SMEM = pl.BlockSpec(memory_space=pltpu.SMEM)
VMEM = pl.BlockSpec(memory_space=pltpu.VMEM)


def shifted(block, axis, distance):
    devices = range(lax.axis_size(axis))
    route = [(i - distance, i) for i in devices if i - distance in devices]
    return lax.ppermute(block, axis, route)


def swapped(block, axis, first):
    count = lax.axis_size(axis)
    pairs = [(i, i + 1) for i in range(first, count - 1, 2)]
    return lax.ppermute(block, axis, pairs + [(b, a) for a, b in pairs])


def columns(head, dim):
    return pl.ds(pl.multiple_of(head * dim, dim), dim)


def dot_nt(a, b):
    return lax.dot_general(a, b, (((1,), (1,)), ((), ())), preferred_element_type=F32)


def dot_nn(a, b):
    return lax.dot_general(a, b, (((1,), (0,)), ((), ())), preferred_element_type=F32)


def dot_tn(a, b):
    return lax.dot_general(a, b, (((0,), (0,)), ((), ())), preferred_element_type=F32)


class Geometry:
    def __init__(self, tokens, width, dim):
        self.tokens, self.width, self.dim = tokens, width, dim
        self.half = tokens // 2
        self.scale = 1.0 / math.sqrt(dim)
        self.frames = lax.axis_size("frame")
        self.frame = lax.axis_index("frame")
        self.row = lax.axis_index("row")
        self.rows = lax.axis_size("row")
        self.even = lax.rem(self.row, 2) == 0
        self.low_lanes = lax.broadcasted_iota(jnp.int32, (1, tokens), 1) < self.half

    def has(self, frame):
        return (frame >= 0) & (frame < self.frames)

    def offsets(self, offs_ref, frame):
        frame = jnp.clip(frame, 0, self.frames - 1)
        first, second = offs_ref[frame, 0], offs_ref[frame, 1]
        lost0 = (first == -1) & (self.row == 0)
        lost1 = (second == 0) & (self.row == self.rows - 1)
        fine, gone = jnp.float32(0.0), jnp.float32(-1e30)
        penalty = jnp.where(
            self.low_lanes, jnp.where(lost0, gone, fine), jnp.where(lost1, gone, fine)
        )
        return first == -1, second == -1, penalty

    def rims(self, near, far):
        return jnp.where(self.even, far, near), jnp.where(self.even, near, far)

    def keys(self, main, low, high, offs):
        half, width = self.half, self.width
        edge0 = jnp.where(offs[0], low, main[half : half + width])
        edge1 = jnp.where(offs[1], main[half - width : half], high)
        return jnp.concatenate([main, edge0, edge1], axis=0)

    def keys_of(self, extended, offs):
        width, end = self.width, self.width + self.tokens
        return self.keys(extended[width:end], extended[:width], extended[end:], offs)

    def by_tile(self, product):
        half, width, tokens = self.half, self.width, self.tokens
        own = jnp.where(self.low_lanes, product[:half], product[half:tokens])
        edge = jnp.where(
            self.low_lanes, product[tokens : tokens + width], product[tokens + width :]
        )
        return own, edge

    def scores(self, keys, values, query, grad, offs):
        own, edge = self.by_tile(dot_nt(keys, query))
        s = jnp.concatenate([own * self.scale, edge * self.scale + offs[2]], axis=0)
        dp = jnp.concatenate(self.by_tile(dot_nt(values, grad)), axis=0)
        return s, dp

    def spread(self, terms):
        half = self.half
        own, edge = terms[:half], terms[half:]
        zero_own, zero_edge = jnp.zeros_like(own), jnp.zeros_like(edge)
        low = self.low_lanes
        return jnp.concatenate(
            [
                jnp.where(low, own, zero_own).astype(BF16),
                jnp.where(low, zero_own, own).astype(BF16),
                jnp.where(low, edge, zero_edge).astype(BF16),
                jnp.where(low, zero_edge, edge).astype(BF16),
            ],
            axis=0,
        )

    def weigh(self, s, dp, top, inverse, delta):
        p = jnp.exp(s - top) * inverse
        ds = p * (dp - delta) * self.scale
        return self.spread(p), self.spread(ds)

    def fold(self, term, offs):
        half, width, tokens = self.half, self.width, self.tokens
        edge0, edge1 = term[tokens : tokens + width], term[tokens + width :]
        none = jnp.zeros_like(edge0)
        return jnp.concatenate(
            [
                jnp.where(offs[0], edge0, none),
                term[: half - width],
                term[half - width : half] + jnp.where(offs[1], edge1, none),
                term[half : half + width] + jnp.where(offs[0], none, edge0),
                term[half + width : tokens],
                jnp.where(offs[1], none, edge1),
            ],
            axis=0,
        )


def stats_of(s, dp):
    top = jnp.max(s, axis=0, keepdims=True)
    expo = jnp.exp(s - top)
    return top, jnp.sum(expo, axis=0, keepdims=True), jnp.sum(expo * dp, axis=0, keepdims=True)


def put_stats(ref, pair, side, stats):
    for j, row in enumerate(stats):
        ref[pair, pl.ds(4 * side + j, 1), :] = row


def get_stats(ref, pair, side):
    return [ref[pair, pl.ds(4 * side + j, 1), :] for j in range(3)]


def merge(first, others, valid):
    low = jnp.float32(-1e30)
    tops = [first[0]] + [jnp.where(ok, o[0], low) for o, ok in zip(others, valid)]
    top = functools.reduce(jnp.maximum, tops)
    factor = jnp.exp(first[0] - top)
    total, weighted = first[1] * factor, first[2] * factor
    for o, ok, t in zip(others, valid, tops[1:]):
        factor = jnp.where(ok, jnp.exp(t - top), jnp.float32(0.0))
        total, weighted = total + o[1] * factor, weighted + o[2] * factor
    inverse = 1.0 / total
    return top, inverse, weighted * inverse


def each(count, body):
    def step(i, carry):
        body(i)
        return carry

    lax.fori_loop(0, count, step, 0)


def edge_kernel(heads, reach, k_first, k_last, v_first, v_last, order, near, far):
    even = lax.rem(lax.axis_index("row"), 2) == 0
    for j, (first, last) in enumerate(((k_first, k_last), (v_first, v_last))):
        near[j] = jnp.where(even, last[...], first[...])
        far[j] = jnp.where(even, first[...], last[...])
    count = lax.fori_loop(0, heads, lambda h, c: c + reach[h], 0)

    def place(h, carry):
        on, off = carry
        hit = reach[h] == 1
        order[jnp.where(hit, on, off)] = h
        return jnp.where(hit, on + 1, on), jnp.where(hit, off, off + 1)

    lax.fori_loop(0, heads, place, (0, count))


def edge_rows(k, v, reach, width):
    tokens, packed = k.shape
    first = pl.BlockSpec((width, packed), lambda i: (0, 0))
    last = pl.BlockSpec((width, packed), lambda i: (tokens // width - 1, 0))
    rim = jax.ShapeDtypeStruct((2, width, packed), BF16)
    whole = pl.BlockSpec((2, width, packed), lambda i: (0, 0, 0))
    return pl.pallas_call(
        functools.partial(edge_kernel, reach.shape[0]),
        grid=(1,),
        out_shape=[jax.ShapeDtypeStruct(reach.shape, jnp.int32), rim, rim],
        in_specs=[SMEM, first, last, first, last],
        out_specs=[SMEM, whole, whole],
        compiler_params=pltpu.CompilerParams(vmem_limit_bytes=VMEM_LIMIT),
        name="edge",
    )(reach, k, k, v, v)


def pack_kernel(n, dim, order, q, g, send):
    def pack(slot):
        cols = columns(order[slot], dim)
        send[slot, 0] = q[:, cols]
        send[slot, 1] = g[:, cols]

    each(n, pack)


def extend_kernel(n, dim, width, order, k, v, near, far, send):
    tokens = k.shape[0]
    geo = Geometry(tokens, width, dim)

    for slot in range(n):
        cols = columns(order[slot], dim)
        for j, ref in enumerate((k, v)):
            low, high = geo.rims(near[j, :, cols], far[j, :, cols])
            send[slot, j, :width] = low
            send[slot, j, width : width + tokens] = ref[:, cols]
            send[slot, j, width + tokens :] = high


def own_kernel(n, heads, dim, width, order, offs, q, g, k, v, near, far, grads, rims):
    tokens = q.shape[0]
    geo = Geometry(tokens, width, dim)
    where = geo.offsets(offs, geo.frame)

    def finish(i):
        cols = columns(order[n + i], dim)
        low, high = geo.rims(near[0, :, cols], far[0, :, cols])
        keys = geo.keys(k[:, cols], low, high, where)
        low, high = geo.rims(near[1, :, cols], far[1, :, cols])
        values = geo.keys(v[:, cols], low, high, where)
        query, grad = q[:, cols], g[:, cols]
        s, dp = geo.scores(keys, values, query, grad, where)
        top, total, weighted = stats_of(s, dp)
        inverse = 1.0 / total
        weights, dscores = geo.weigh(s, dp, top, inverse, weighted * inverse)
        grads[i, 0] = dot_tn(dscores, keys).astype(BF16)
        for j, term in enumerate((dot_nn(dscores, query), dot_nn(weights, grad))):
            folded = geo.fold(term, where)
            grads[i, 1 + j] = folded[width : width + tokens].astype(BF16)
            rims[i, 0, j] = folded[:width].astype(BF16)
            rims[i, 1, j] = folded[width + tokens :].astype(BF16)

    each(heads - n, finish)


def query_kernel(n, dim, width, order, reach, offs, own_q, own, prev, following, stats, s_out, dp_out):
    geo = Geometry(own_q.shape[2], width, dim)
    where = geo.offsets(offs, geo.frame)
    has_prev, has_next = geo.has(geo.frame - 1), geo.has(geo.frame + 1)

    def pair_step(pair, carry):
        for side in range(2):
            slot = 2 * pair + side
            on = reach[order[slot]] == 1
            parts = []
            for i, block in enumerate((own, prev, following)):
                keys = geo.keys_of(block[slot, 0], where)
                values = geo.keys_of(block[slot, 1], where)
                s, dp = geo.scores(keys, values, own_q[slot, 0], own_q[slot, 1], where)
                s_out[slot, i] = s
                dp_out[slot, i] = dp
                parts.append(stats_of(s, dp))
            put_stats(stats, pair, side, merge(parts[0], parts[1:], [on & has_prev, on & has_next]))
        return carry

    lax.fori_loop(0, n // 2, pair_step, 0)


def finish_kernel(
    n, dim, width, order, reach, offs, own_q, own, prev, following, stats, s_in, dp_in, acc, dq
):
    geo = Geometry(own_q.shape[2], width, dim)
    where = geo.offsets(offs, geo.frame)
    has_prev, has_next = geo.has(geo.frame - 1), geo.has(geo.frame + 1)

    def pair_step(pair, carry):
        for side in range(2):
            slot = 2 * pair + side
            on = reach[order[slot]] == 1
            top, inverse, delta = get_stats(stats, pair, side)
            total = None
            for i, (block, ok) in enumerate(
                ((own, None), (prev, on & has_prev), (following, on & has_next))
            ):
                keys = geo.keys_of(block[slot, 0], where)
                part = inverse if ok is None else jnp.where(ok, inverse, jnp.float32(0.0))
                s = s_in[slot, i] if ok is None else jnp.minimum(s_in[slot, i], top)
                weights, dscores = geo.weigh(s, dp_in[slot, i], top, part, delta)
                term = dot_tn(dscores, keys)
                total = term if total is None else total + term
                if ok is None:
                    acc[slot, 0] = geo.fold(dot_nn(dscores, own_q[slot, 0]), where)
                    acc[slot, 1] = geo.fold(dot_nn(weights, own_q[slot, 1]), where)
            dq[slot] = total.astype(BF16)
        return carry

    lax.fori_loop(0, n // 2, pair_step, 0)


def key_kernel(
    n, dim, width, order, reach, offs, own, q_prev, q_next, st_prev, st_next, acc, *refs
):
    tokens = q_prev.shape[2]
    geo = Geometry(tokens, width, dim)
    half, end = tokens // 2, width + tokens
    others, (grads, rim_near, rim_far) = refs[:-3], refs[-3:]
    places = [geo.offsets(offs, geo.frame + step) for step in (-1, 1)]
    penalty = jnp.concatenate([place[2] for place in places], axis=1)
    lane = lax.broadcasted_iota(jnp.int32, (1, 2 * tokens), 1)
    first_tile = lax.rem(lane, tokens) < half
    quarters = [(lane >= i * half) & (lane < (i + 1) * half) for i in range(4)]

    def rows_of(extended):
        main = extended[width:end]
        rows = [main]
        for place in places:
            rows.append(jnp.where(place[0], extended[:width], main[half : half + width]))
            rows.append(jnp.where(place[1], main[half - width : half], extended[end:]))
        return jnp.concatenate(rows, axis=0)

    def by_tile(product):
        main = jnp.where(first_tile, product[:half], product[half:tokens])
        edges = []
        for i in range(2):
            at = tokens + 2 * i * width
            lanes = slice(i * tokens, (i + 1) * tokens)
            edges.append(
                jnp.where(
                    geo.low_lanes,
                    product[at : at + width, lanes],
                    product[at + width : at + 2 * width, lanes],
                )
            )
        return main, jnp.concatenate(edges, axis=1)

    def spread(terms):
        main, edge = terms[:half], terms[half:]
        zero = jnp.zeros_like(main)
        rows = [jnp.where(first_tile, main, zero), jnp.where(first_tile, zero, main)]
        rows += [jnp.where(quarter, edge, jnp.zeros_like(edge)) for quarter in quarters]
        return jnp.concatenate([row.astype(BF16) for row in rows], axis=0)

    def fold(term, base):
        low, main, high = base[:width], base[width:end], base[end:]
        up, down = main[half - width : half], main[half : half + width]
        for i, place in enumerate(places):
            at = tokens + 2 * i * width
            edge0, edge1 = term[at : at + width], term[at + width : at + 2 * width]
            none = jnp.zeros_like(edge0)
            low = low + jnp.where(place[0], edge0, none)
            down = down + jnp.where(place[0], none, edge0)
            up = up + jnp.where(place[1], edge1, none)
            high = high + jnp.where(place[1], none, edge1)
        main = jnp.concatenate([main[: half - width], up, down, main[half + width :]], axis=0)
        return low, main + term[:tokens], high

    def pair_step(pair):
        for side in range(2):
            slot = 2 * pair + side
            head = order[slot]
            on = reach[head] == 1
            query = jnp.concatenate([q_prev[slot, 0], q_next[slot, 0]], axis=0)
            grad = jnp.concatenate([q_prev[slot, 1], q_next[slot, 1]], axis=0)
            main, edge = by_tile(dot_nt(rows_of(own[slot, 0]), query))
            s = jnp.concatenate([main * geo.scale, edge * geo.scale + penalty], axis=0)
            dp = jnp.concatenate(by_tile(dot_nt(rows_of(own[slot, 1]), grad)), axis=0)
            columns_of = []
            for step, stats in ((-1, st_prev), (1, st_next)):
                top, inverse, delta = get_stats(stats, pair, side)
                ok = on & geo.has(geo.frame + step)
                columns_of.append((top, jnp.where(ok, inverse, jnp.float32(0.0)), delta))
            top, inverse, delta = (jnp.concatenate(x, axis=1) for x in zip(*columns_of))
            p = jnp.exp(jnp.minimum(s, top) - top) * inverse
            ds = p * (dp - delta) * geo.scale
            cols = columns(head, dim)
            for j, term in enumerate((dot_nn(spread(ds), query), dot_nn(spread(p), grad))):
                low, main, high = fold(term, acc[slot, j])
                grads[slot, j] = main.astype(BF16)
                put_rims(geo, rim_near, rim_far, j, cols, low.astype(BF16), high.astype(BF16))

    each(n // 2, pair_step)
    if others:
        spread_rims(geo, n, order, others[0], rim_near, rim_far)


def put_rims(geo, near, far, j, cols, low, high):
    near[j, :, cols] = jnp.where(geo.even, high, low)
    far[j, :, cols] = jnp.where(geo.even, low, high)


def spread_rims(geo, n, order, rims, near, far):
    def put(i):
        cols = columns(order[n + i], geo.dim)
        for j in range(2):
            put_rims(geo, near, far, j, cols, rims[i, 0, j], rims[i, 1, j])

    each(rims.shape[0], put)


def query_out_kernel(n, dim, order, *refs):
    parts, out = refs[:-1], refs[-1]

    def active(slot):
        out[:, columns(order[slot], dim)] = parts[0][slot]

    def passive(i):
        out[:, columns(order[n + i], dim)] = parts[1][i, 0]

    each(n, active)
    if len(parts) > 1:
        each(parts[1].shape[0], passive)


def last_kernel(n, dim, width, order, near, far, *refs):
    parts, outs = refs[:-2], refs[-2:]
    tokens = outs[0].shape[0]
    geo = Geometry(tokens, width, dim)

    def put(j, head, ref, i, at):
        cols = columns(head, dim)
        out = outs[j]
        below, above = geo.rims(near[j, :, cols], far[j, :, cols])
        low = ref[i, at, :width].astype(F32) + below.astype(F32)
        high = ref[i, at, tokens - width :].astype(F32) + above.astype(F32)
        out[:width, cols] = low.astype(BF16)
        out[width : tokens - width, cols] = ref[i, at, width : tokens - width]
        out[tokens - width :, cols] = high.astype(BF16)

    def active(slot):
        for j in range(2):
            put(j, order[slot], parts[0], slot, j)

    def passive(i):
        for j in range(2):
            put(j, order[n + i], parts[1], i, 1 + j)

    each(n, active)
    if len(parts) > 1:
        each(parts[1].shape[0], passive)


def call(name, kernel, ins, outs, flops):
    shapes = [jax.ShapeDtypeStruct(s, d) for s, d in outs]
    moved = sum(x.size * x.dtype.itemsize for x in list(ins) + shapes)
    return pl.pallas_call(
        kernel,
        out_shape=shapes,
        in_specs=[SMEM if x.dtype == jnp.int32 else VMEM for x in ins],
        out_specs=[SMEM if x.dtype == jnp.int32 else VMEM for x in shapes],
        cost_estimate=pl.CostEstimate(flops=flops, bytes_accessed=moved, transcendentals=0),
        compiler_params=pltpu.CompilerParams(vmem_limit_bytes=VMEM_LIMIT),
        name=name,
    )(*ins)


def run(n, heads, dim, width, args):
    q, g, k, v, reach, offs, order, near, far = args
    tokens, packed = q.shape
    part = functools.partial
    rim = ((2, width, packed), BF16)
    whole = ((tokens, packed), BF16)
    tile = (tokens, dim)
    longer = (tokens + 2 * width, dim)
    flops = 2 * longer[0] * tokens * dim
    rest = heads - n
    (own,) = call(
        "extend", part(extend_kernel, n, dim, width), [order, k, v, near, far],
        [((n, 2) + longer, BF16)], 0,
    )
    prev, following = shifted(own, "frame", 1), shifted(own, "frame", -1)
    (own_q,) = call("pack", part(pack_kernel, n, dim), [order, q, g], [((n, 2) + tile, BF16)], 0)
    q_prev, q_next = shifted(own_q, "frame", 1), shifted(own_q, "frame", -1)
    more, rims = [], []
    if rest:
        grads_own, rims_own = call(
            "own", part(own_kernel, n, heads, dim, width), [order, offs, q, g, k, v, near, far],
            [((rest, 3) + tile, BF16), ((rest, 2, 2, width, dim), BF16)], flops * 5 * rest,
        )
        more, rims = [grads_own], [rims_own]
    grid = ((n, 3, tokens // 2 + width, tokens), F32)
    stats, s, dp = call(
        "query", part(query_kernel, n, dim, width),
        [order, reach, offs, own_q, own, prev, following],
        [((n // 2, 8, tokens), F32), grid, grid], flops * 6 * n,
    )
    st_prev, st_next = shifted(stats, "frame", 1), shifted(stats, "frame", -1)
    acc, dq = call(
        "finish", part(finish_kernel, n, dim, width),
        [order, reach, offs, own_q, own, prev, following, stats, s, dp],
        [((n, 2) + longer, F32), ((n,) + tile, BF16)], flops * 5 * n,
    )
    grads, rim_near, rim_far = call(
        "key", part(key_kernel, n, dim, width),
        [order, reach, offs, own, q_prev, q_next, st_prev, st_next, acc] + rims,
        [((n, 2) + tile, BF16), rim, rim], flops * 8 * n,
    )
    near, far = swapped(rim_near, "row", 0), swapped(rim_far, "row", 1)
    (dq,) = call("dq", part(query_out_kernel, n, dim), [order, dq] + more, [whole], 0)
    dk, dv = call(
        "last", part(last_kernel, n, dim, width), [order, near, far, grads] + more,
        [whole, whole], 0,
    )
    return dq, dk, dv


def on_device(query_tok, key_tok, value_tok, grad_out, head_reach, tile_offset):
    block = query_tok.shape
    rows_dev, width, packed = block[1:]
    heads = head_reach.shape[0]
    dim = packed // heads
    flat = [x.reshape(rows_dev * width, packed) for x in (query_tok, grad_out, key_tok, value_tok)]
    order, near, far = edge_rows(flat[2], flat[3], head_reach, width)
    near, far = swapped(near, "row", 0), swapped(far, "row", 1)
    args = flat + [head_reach, tile_offset, order, near, far]
    sizes = [min(n, heads) for n in SIZES]
    count = jnp.sum(head_reach)
    grads = lax.switch(
        lax.shift_right_arithmetic(count - (SIZES[0] - 1), 1),
        [functools.partial(run, n, heads, dim, width) for n in sizes],
        args,
    )
    return tuple(x.reshape(block) for x in grads)


def solution(mesh):
    spec = P("frame", "row", None, None)
    return jax.shard_map(
        on_device,
        mesh=mesh,
        in_specs=(spec, spec, spec, spec, P(), P(None, "row")),
        out_specs=(spec, spec, spec),
        check_vma=False,
    )
```
